32 devices in a mesh: fsdp: 8 (over y, x, core), group: 4 (over z).
Axes of the slice: x: 2, y: 2, z: 4, core: 2. Of those that a mesh axis runs over, the one named last changes fastest.
Arguments:
- gradient: bfloat16 [4, 512, 4096], P('group', 'fsdp'), may hold values from -4000 to 4000
- first_moment: bfloat16 [4, 4096, 512], P('group', 'fsdp'), may hold values from -3 to 3
- second_moment: bfloat16 [4, 4096, 512], P('group', 'fsdp'), may hold values from 0.29882812 to 3
- basis_store: bfloat16 [4, 4608, 256], P('group', 'fsdp'), may hold values from -1 to 2
- step_number: int32 [1], replicated, may hold values from 1 to 99999
- matrix_ids: int32 [4], P('group'), may hold values from 0 to 3, each once
Outputs:
- update: bfloat16 [4, 512, 4096], P('group', 'fsdp')
- new_first: bfloat16 [4, 4096, 512], P('group', 'fsdp')
- new_second: bfloat16 [4, 4096, 512], P('group', 'fsdp')
The draws below stay inside these ranges and needn't reach their ends.
Inputs may be any that keep to these rules, and one draw needn't show every extreme that they name: `matrix_ids`: each matrix index once.
All inputs are finite; a program needn't handle non-finite values.
Results may differ from the reference program's by a relative error of at most 0.0004.
Values may be sent and summed in bfloat16 or wider, within the bound.
A program may use at most 64 MiB of HBM per device.

```python
import math
import jax
import jax.numpy as jnp
from jax import lax

COLS = 4096
BLOCK = 256
ROWS = 512
MATS = 4
BROWS = 4608
OWNER_ROWS = 576
LEFT_BLOCKS = 2
RIGHT_BLOCKS = 16
ELEMS = 8388608
N_FSDP = 8


def draw_gradient(key, part):
    key_base, key_cols = jax.random.split(key, 2)
    place = jnp.arange(ROWS, dtype=jnp.float32) / ROWS
    col_scale = jnp.exp(jax.random.uniform(key_cols, (COLS,), jnp.float32, 0.0, math.log(10.0)))
    mat_scale = 1.0 + 2.0 * jnp.arange(MATS, dtype=jnp.float32) / max(MATS - 1, 1)
    base = jax.random.truncated_normal(key_base, -6.0, 6.0, (MATS, ROWS, COLS), jnp.float32)
    row_scale = jnp.power(10.0, place)
    values = 2.0 * base * mat_scale[:, None, None] * row_scale[None, :, None] * col_scale[None, None, :]
    return values.astype(jnp.bfloat16)


def draw_basis_store(key, part):
    noise = jax.random.truncated_normal(key, -6.0, 6.0, (MATS, BROWS, BLOCK), jnp.float32)
    noise = noise * (0.25 / math.sqrt(BLOCK))
    unit = (jnp.arange(BROWS)[:, None] % BLOCK == jnp.arange(BLOCK)[None, :]).astype(jnp.float32)
    return (unit[None, :, :] + noise).astype(jnp.bfloat16)


def steps_of(stream_key, shape, pieces, least, largest):
    loudness = 1.0
    for position, parts in pieces:
        heights = jax.random.uniform(jax.random.fold_in(jax.random.fold_in(stream_key, 6), position), (parts,), jnp.float32, least / len(pieces), largest / len(pieces))
        loudness = loudness * jnp.repeat(jnp.exp(heights), shape[position] // parts).reshape((-1,) + (1,) * (len(shape) - 1 - position))
    return loudness


def gaussian(key, extent, deviation, limit, cuts=(), kind=jnp.bfloat16):
    entries = deviation * jax.random.normal(key, extent, jnp.float32)
    if cuts:
        entries = entries * steps_of(key, extent, cuts, -0.22, 0.18)
    return jnp.clip(entries, -limit, limit).astype(kind)


def setup_inputs(seed: int = 0) -> dict:
    streams_of = jax.random.split(jax.random.key(seed), 7)
    gradient = draw_gradient(jax.random.fold_in(streams_of[6], 71), 0)
    first_moment = gaussian(streams_of[1], (MATS, COLS, ROWS), 0.5, 3.0, ((0, 4), (1, 8)))
    second_moment = jnp.clip(jnp.exp(math.log(3.0) - 2.306499 * jax.random.uniform(streams_of[2], (MATS, COLS, ROWS), jnp.float32) ** steps_of(streams_of[2], (MATS, COLS, ROWS), ((0, 4), (1, 8)), -0.2, 0.2)), 0.29882812, 3.0).astype(jnp.bfloat16)
    basis_store = draw_basis_store(jax.random.fold_in(streams_of[6], 71), 0)
    step_number = jax.random.randint(streams_of[4], (1,), 1, 100000).astype(jnp.int32)
    matrix_ids = jax.random.permutation(streams_of[5], MATS).astype(jnp.int32)
    return {"gradient": gradient, "first_moment": first_moment, "second_moment": second_moment, "basis_store": basis_store, "step_number": step_number, "matrix_ids": matrix_ids}


BETA_ONE = 0.95
BETA_TWO = 0.95
ADAM_EPS = 1e-08
HIGHEST = lax.Precision.HIGHEST

def reference(gradient, first_moment, second_moment, basis_store, step_number, matrix_ids):
    total = jnp.float32(0.0)
    for index in range(MATS):
        single = gradient[index].astype(jnp.float32)
        total = total + jnp.sum(single * single)
    clip = jnp.sqrt(jnp.float32(ELEMS)) / (jnp.sqrt(total) + 1e-06)
    count = step_number[0].astype(jnp.float32)
    first_fix = 1.0 - jnp.power(jnp.float32(BETA_ONE), count)
    second_fix = 1.0 - jnp.power(jnp.float32(BETA_TWO), count)
    updates = []
    firsts = []
    seconds = []
    for index in range(MATS):
        shift = ((step_number[0] + matrix_ids[index]) % N_FSDP).astype(jnp.int32) * OWNER_ROWS
        ordered = jnp.roll(basis_store[index], -shift, axis=0).astype(jnp.float32)
        left = ordered[:ROWS].reshape(LEFT_BLOCKS, BLOCK, BLOCK)
        right = ordered[ROWS:].reshape(RIGHT_BLOCKS, BLOCK, BLOCK)
        plain = gradient[index].astype(jnp.float32)
        turned = jnp.einsum('rbj,bjl->rbl', plain.reshape(ROWS, RIGHT_BLOCKS, BLOCK), right, precision=HIGHEST).reshape(ROWS, COLS)
        turned = clip * turned
        rotated = jnp.einsum('bkc,bki->cbi', turned.reshape(LEFT_BLOCKS, BLOCK, COLS), left, precision=HIGHEST).reshape(COLS, ROWS)
        first_sum = BETA_ONE * first_moment[index].astype(jnp.float32) + (1.0 - BETA_ONE) * rotated
        second_sum = BETA_TWO * second_moment[index].astype(jnp.float32) + (1.0 - BETA_TWO) * rotated * rotated
        direction = first_sum / first_fix / (jnp.sqrt(second_sum / second_fix) + ADAM_EPS)
        backward = jnp.einsum('cbi,bki->cbk', direction.reshape(COLS, LEFT_BLOCKS, BLOCK), left, precision=HIGHEST).reshape(COLS, ROWS)
        result = jnp.einsum('blr,bjl->rbj', backward.reshape(RIGHT_BLOCKS, BLOCK, ROWS), right, precision=HIGHEST).reshape(ROWS, COLS)
        updates.append(result.astype(jnp.bfloat16))
        firsts.append(first_sum.astype(jnp.bfloat16))
        seconds.append(second_sum.astype(jnp.bfloat16))
    return (jnp.stack(updates), jnp.stack(firsts), jnp.stack(seconds))
```

```python
import functools
import math

import jax
import jax.numpy as jnp
from jax import lax
from jax.experimental import pallas as pl
from jax.experimental.pallas import tpu as pltpu
from jax.sharding import PartitionSpec as P

BLOCK = 256


BETA_ONE = 0.95
BETA_TWO = 0.95
ADAM_EPS = 1e-08
HIGHEST = lax.Precision.HIGHEST


def clip_of(local_squares, entries):
    total = lax.psum(local_squares, ("fsdp", "group"))
    return jnp.float32(math.sqrt(entries)) / (jnp.sqrt(total) + 1e-06)


def local_general(gradient, first_moment, second_moment, basis_store, step_number, matrix_ids):
    fsdp_count = lax.axis_size("fsdp")
    group_count = lax.axis_size("group")
    row_count = gradient.shape[1]
    col_count = gradient.shape[2]
    all_rows = row_count * fsdp_count
    col_share = col_count // fsdp_count
    left_blocks = all_rows // BLOCK
    right_blocks = col_count // BLOCK
    entries = all_rows * col_count * group_count
    grad_local = gradient[0].astype(jnp.float32)
    local_squares = jnp.sum(grad_local * grad_local)
    gathered = lax.all_gather(basis_store[0], "fsdp", axis=0, tiled=True)
    owner_rows = basis_store.shape[1]
    owner = (step_number[0] + matrix_ids[0]) % fsdp_count
    ordered_half = jnp.roll(gathered, -owner * owner_rows, axis=0)
    left = ordered_half[:all_rows].astype(jnp.float32).reshape(left_blocks, BLOCK, BLOCK)
    right_half = ordered_half[all_rows:].reshape(right_blocks, BLOCK, BLOCK)
    right = right_half.astype(jnp.float32)
    turned = jnp.einsum(
        "rbj,bjl->rbl",
        gradient[0].reshape(row_count, right_blocks, BLOCK),
        right_half,
        preferred_element_type=jnp.float32,
    )
    turned = clip_of(local_squares, entries) * turned
    outgoing = turned.reshape(row_count, fsdp_count, col_share)
    received = lax.all_to_all(outgoing, "fsdp", split_axis=1, concat_axis=0, tiled=True)
    width = received.shape[2]
    columns = received[:, 0, :].reshape(left_blocks, BLOCK, width)
    rotated = jnp.einsum("bkc,bki->cbi", columns, left, precision=HIGHEST).reshape(width, all_rows)
    count = step_number[0].astype(jnp.float32)
    first_fix = 1.0 - jnp.power(jnp.float32(BETA_ONE), count)
    second_fix = 1.0 - jnp.power(jnp.float32(BETA_TWO), count)
    first_sum = BETA_ONE * first_moment[0].astype(jnp.float32) + (1.0 - BETA_ONE) * rotated
    second_sum = (
        BETA_TWO * second_moment[0].astype(jnp.float32) + (1.0 - BETA_TWO) * rotated * rotated
    )
    direction = first_sum / first_fix / (jnp.sqrt(second_sum / second_fix) + ADAM_EPS)
    backward = jnp.einsum(
        "cbi,bki->cbk", direction.reshape(col_share, left_blocks, BLOCK), left, precision=HIGHEST
    )
    returning = backward.reshape(col_share, fsdp_count, row_count)
    received = lax.all_to_all(returning, "fsdp", split_axis=1, concat_axis=0, tiled=True)
    width = received.shape[2]
    pieces = received[:, 0, :].reshape(right_blocks, BLOCK, width)
    result = jnp.einsum("blr,bjl->rbj", pieces, right, precision=HIGHEST).reshape(width, col_count)
    return (
        result[None].astype(jnp.bfloat16),
        first_sum[None].astype(jnp.bfloat16),
        second_sum[None].astype(jnp.bfloat16),
    )


SLAB = 16
LANES = 128
PARTS = 1
MESH = pl.DeviceIdType.MESH


def pieces_of(x):
    high = x.astype(jnp.bfloat16)
    rest = x - high.astype(jnp.float32)
    middle = rest.astype(jnp.bfloat16)
    low = (rest - middle.astype(jnp.float32)).astype(jnp.bfloat16)
    return high, middle, low


def mm(a, b, dims):
    return lax.dot_general(a, b, (dims, ((), ())), preferred_element_type=jnp.float32)


NN = ((1,), (0,))
NT = ((1,), (1,))


def kernel(n, groups, grad, first, second, basis, step, ident, out_u, out_1, out_2,
           own, moments, hop, staged, left, right, got, upd, sq_own, sq_z, sq_mid, sq_f,
           loc, hop_s, hop_r, left_s, left_r, right_s, right_r, got_s, got_r,
           ret_s, ret_r, z_s, z_r, f_s, f_r):
    me = lax.axis_index("fsdp")
    zz = lax.axis_index("group")
    share = grad.shape[1]
    cols = grad.shape[2]
    width = cols // n
    halves = width // BLOCK
    slabs = n // 2
    per_owner = basis.shape[0]
    span = slabs * SLAB
    left_groups = left.shape[0]
    all_rows = share * n
    left_blocks = all_rows // BLOCK
    block_groups = BLOCK // span
    entries = float(share * n * cols * groups)

    core = lax.rem(me, 2)
    per = n // left_blocks
    masks = [m for m in range(2, n, 2)] + [m for m in range(3, n, 2)]
    swapped = [masks[i + 1] if i % 2 == 0 and i + 1 < len(masks) else masks[i - i % 2] for i in range(len(masks))]
    order = list(zip(masks, swapped)) + [(1, 1)]

    def peer(m):
        other = me
        for bit in (1 << i for i in range(n.bit_length() - 1)):
            if m & bit:
                other = other + bit * (1 - 2 * lax.rem(me // bit, 2))
        return other

    def pick(pair):
        a, b = pair
        return a + core * (b - a), peer(a) + core * (peer(b) - peer(a))

    def zpeer(k):
        return lax.rem(zz + k, groups)

    def lanes_of(c):
        return pl.ds(pl.multiple_of(lax.rem(c, 2) * LANES, LANES), LANES)

    def rows_of(c):
        return pl.ds(pl.multiple_of((c // 2) * SLAB, SLAB), SLAB)

    def share_rows(d):
        return pl.ds(pl.multiple_of(d * share, share), share)

    def out_cols(d, t):
        return pl.ds(pl.multiple_of(d * width + t * BLOCK, BLOCK), BLOCK)

    def settle(ref, sem):
        pltpu.make_async_copy(ref, ref, sem).wait()

    def remote(src, dst, ssem, rsem, d):
        return pltpu.make_async_remote_copy(
            src_ref=src, dst_ref=dst, send_sem=ssem, recv_sem=rsem,
            device_id={"fsdp": d}, device_id_type=MESH)

    locals_ = [
        pltpu.make_async_copy(grad.at[0], own, loc.at[0]),
        pltpu.make_async_copy(basis.at[:, me // 2, :, lanes_of(me)], hop.at[me], hop_r),
        pltpu.make_async_copy(first.at[0], moments.at[0], loc.at[1]),
        pltpu.make_async_copy(second.at[0], moments.at[1], loc.at[1]),
    ]
    for t in range(halves):
        locals_.append(pltpu.make_async_copy(
            grad.at[0, :, out_cols(me, t)], got.at[t, share_rows(me)], got_r.at[t, 0]))
    for copy in locals_:
        copy.start()

    barrier = pltpu.get_barrier_semaphore()
    for k in range(1, n):
        pl.semaphore_signal(barrier, inc=1, device_id={"fsdp": peer(k)}, device_id_type=MESH)
    for k in range(1, groups):
        pl.semaphore_signal(barrier, inc=1, device_id={"group": zpeer(k)}, device_id_type=MESH)
    pl.semaphore_wait(barrier, n - 1 + groups - 1)

    def hop_copy(m, d):
        return remote(basis.at[:, d // 2, :, lanes_of(d)], hop.at[me], hop_s, hop_r, d)

    def got_copy(t, m, d):
        return remote(own.at[:, out_cols(d, t)], got.at[t, share_rows(me)],
                      got_s, got_r.at[t, m // per], d)

    def right_copy(t, m, d):
        src = staged.at[pl.ds(left_groups + (d * halves + t) * block_groups, block_groups)]
        dst = right.at[t, :, rows_of(me), lanes_of(me)]
        return remote(src, dst, right_s, right_r.at[t], d)

    def left_copy(m, d):
        return remote(staged.at[pl.ds(0, left_groups)], left.at[:, rows_of(me), lanes_of(me)],
                      left_s.at[0], left_r.at[0], d)

    for pair in order:
        hop_copy(*pick(pair)).start()
    shared = left.at[:, :, lanes_of(me)]
    sibling = remote(shared, shared, left_s.at[1], left_r.at[1], peer(1))

    def send_got(t):
        for pair in order:
            got_copy(t, *pick(pair)).start()

    locals_[0].wait()
    squares = jnp.zeros((8, LANES), jnp.float32)
    for r in range(0, share, 16):
        rows = own[r:r + 16, :].astype(jnp.float32)
        rows = rows * rows
        rows = rows[0:8] + rows[8:16]
        for c in range(0, cols, LANES):
            squares = squares + rows[:, c:c + LANES]
    sq_own[...] = squares
    for k in range(1, groups):
        pltpu.make_async_remote_copy(
            src_ref=sq_own, dst_ref=sq_z.at[k - 1], send_sem=z_s, recv_sem=z_r,
            device_id={"group": zpeer(k)}, device_id_type=MESH).start()

    send_got(0)

    squares = sq_own[...]
    settle(sq_z, z_r)
    for k in range(groups - 1):
        squares = squares + sq_z[k]
    sq_mid[...] = squares
    for k in range(1, n):
        remote(sq_mid, sq_f.at[k - 1], f_s, f_r, peer(k)).start()

    settle(hop, hop_r)
    owner = lax.rem(step[0] + ident[0], n)
    for q in range(n):
        staged[q * per_owner:(q + 1) * per_owner] = hop[lax.rem(owner + q, n)]

    own_left = pltpu.make_async_copy(
        staged.at[pl.ds(0, left_groups)], left.at[:, rows_of(me), lanes_of(me)], left_r.at[0])
    own_left.start()
    for t in range(halves):
        pltpu.make_async_copy(
            staged.at[pl.ds(left_groups + (me * halves + t) * block_groups, block_groups)],
            right.at[t, :, rows_of(me), lanes_of(me)], right_r.at[t]).start()
    lefts_order = [m for m in order if m[0] % 2 == 0]
    def send_right(t):
        for pair in order:
            right_copy(t, *pick(pair)).start()

    send_right(0)
    for m, _ in lefts_order:
        left_copy(m, peer(m)).start()
    for t in range(1, halves):
        send_right(t)
        send_got(t)

    squares = sq_mid[...]
    settle(sq_f, f_r)
    for k in range(n - 1):
        squares = squares + sq_f[k]
    total = jnp.sum(squares, keepdims=True)
    clip = jnp.float32(math.sqrt(entries)) / (jnp.sqrt(total) + 1e-06)
    count = jnp.full((1, 1), step[0].astype(jnp.float32))
    first_inv = 1.0 / (1.0 - jnp.exp(count * jnp.float32(math.log(BETA_ONE))))
    second_inv = 1.0 / (1.0 - jnp.exp(count * jnp.float32(math.log(BETA_TWO))))

    settle(moments, loc.at[1])
    settle(shared, left_r.at[0])
    sibling.start()
    for t in range(halves):
        settle(right.at[t], right_r.at[t])
        rt = right[t].reshape(BLOCK, BLOCK)
        flipped = rt.astype(jnp.float32).T.astype(jnp.bfloat16)
        cut = slice(t * BLOCK, (t + 1) * BLOCK)
        if t == 0:
            sibling.wait_recv()
        for i in reversed(range(left_blocks)):
            b = peer(i * per) // per
            cols_b = pl.ds(pl.multiple_of(b * BLOCK, BLOCK), BLOCK)
            near = range(i * per, (i + 1) * per)
            settle(got.at[t, cols_b], got_r.at[t, i])
            lb = left[pl.ds(b * block_groups, block_groups)].reshape(BLOCK, BLOCK)
            turned = mm(flipped, got[t, cols_b, :], NT)
            rotated = sum(mm(piece, lb, NN) for piece in pieces_of(turned)) * clip
            first_sum = BETA_ONE * moments[0, cut, cols_b].astype(jnp.float32) + (1.0 - BETA_ONE) * rotated
            second_sum = (BETA_TWO * moments[1, cut, cols_b].astype(jnp.float32)
                          + (1.0 - BETA_TWO) * rotated * rotated)
            out_1[0, cut, cols_b] = first_sum.astype(jnp.bfloat16)
            out_2[0, cut, cols_b] = second_sum.astype(jnp.bfloat16)
            direction = first_sum * first_inv / (jnp.sqrt(second_sum * second_inv) + ADAM_EPS)
            back = sum(mm(rt, piece, NN) for piece in pieces_of(direction))
            result = sum(mm(lb, piece, NT) for piece in pieces_of(back))
            upd[t, cols_b, :] = result.astype(jnp.bfloat16)
            for m in reversed(near):
                src = upd.at[t, share_rows(peer(m))]
                dst = out_u.at[0, :, out_cols(me, t)]
                if m == 0:
                    copy = pltpu.make_async_copy(src, dst, ret_r)
                else:
                    copy = remote(src, dst, ret_s, ret_r, peer(m))
                copy.start()

    settle(hop.at[pl.ds(0, n - 1)], hop_s)
    settle(sq_z, z_s)
    settle(sq_f, f_s)
    settle(staged.at[pl.ds(0, (n // 2 - 1) * left_groups)], left_s.at[0])
    sibling.wait_send()
    settle(staged.at[pl.ds(0, (n - 1) * halves * block_groups)], right_s)
    settle(got.at[:, pl.ds(0, all_rows - share)], got_s)
    settle(upd.at[:, pl.ds(0, all_rows - share)], ret_s)
    settle(out_u, ret_r)


def hbm(x):
    return pltpu.with_memory_space_constraint(x, pltpu.MemorySpace.HBM)


def copy_kernel(a, b, c, x, y, z, sems):
    copies = []
    for src, dst in ((a, x), (b, y), (c, z)):
        rows = src.shape[1] // PARTS
        for i in range(PARTS):
            cut = pl.ds(i * rows, rows)
            copies.append(pltpu.make_async_copy(
                src.at[0, cut], dst.at[0, cut], sems.at[len(copies)]))
    for copy in copies:
        copy.start()
    for copy in copies:
        copy.wait()


def place(arrays):
    return pl.pallas_call(
        copy_kernel,
        out_shape=tuple(jax.ShapeDtypeStruct(a.shape, a.dtype) for a in arrays),
        in_specs=[pl.BlockSpec(memory_space=pltpu.VMEM)] * 3,
        out_specs=(pl.BlockSpec(memory_space=pl.ANY),) * 3,
        scratch_shapes=[pltpu.SemaphoreType.DMA((3 * PARTS,))],
        compiler_params=pltpu.CompilerParams(vmem_limit_bytes=8 << 20),
    )(*arrays)


def fits(gradient, first_moment, basis_store, n):
    if n < 2 or n & (n - 1):
        return False
    span = n // 2 * SLAB
    width = gradient.shape[2] // n
    all_rows = gradient.shape[1] * n
    return (
        BLOCK % span == 0
        and basis_store.shape[1] % span == 0
        and width % BLOCK == 0
        and all_rows % BLOCK == 0
        and n % (all_rows // BLOCK) == 0
        and gradient.shape[1] % SLAB == 0
        and all_rows <= 1024
        and width <= 1024
    )


def local(gradient, first_moment, second_moment, basis_store, step_number, matrix_ids):
    n = lax.axis_size("fsdp")
    groups = lax.axis_size("group")
    if not fits(gradient, first_moment, basis_store, n):
        return local_general(
            gradient, first_moment, second_moment, basis_store, step_number, matrix_ids
        )
    share, cols = gradient.shape[1:]
    all_rows = share * n
    width = cols // n
    halves = width // BLOCK
    slabs = n // 2
    span = slabs * SLAB
    per_owner = basis_store.shape[1] // span
    basis = basis_store.reshape(per_owner, slabs, SLAB, BLOCK)
    half = jnp.bfloat16
    anywhere = pl.BlockSpec(memory_space=pl.ANY)
    scalar = pl.BlockSpec(memory_space=pltpu.SMEM)
    dma = pltpu.SemaphoreType.DMA
    tile = (8, LANES)
    results = pl.pallas_call(
        functools.partial(kernel, n, groups),
        out_shape=(
            jax.ShapeDtypeStruct(gradient.shape, half),
            jax.ShapeDtypeStruct(first_moment.shape, half),
            jax.ShapeDtypeStruct(second_moment.shape, half),
        ),
        in_specs=[anywhere] * 4 + [scalar] * 2,
        out_specs=(pl.BlockSpec(memory_space=pltpu.VMEM),) * 3,
        scratch_shapes=[
            pltpu.VMEM((share, cols), half),
            pltpu.VMEM((2, width, all_rows), half),
            pltpu.VMEM((n, per_owner, SLAB, LANES), half),
            pltpu.VMEM((n * per_owner, SLAB, LANES), half),
            pltpu.VMEM((all_rows // span, span, BLOCK), half),
            pltpu.VMEM((halves, BLOCK // span, span, BLOCK), half),
            pltpu.VMEM((halves, all_rows, BLOCK), half),
            pltpu.VMEM((halves, all_rows, BLOCK), half),
            pltpu.VMEM(tile, jnp.float32),
            pltpu.VMEM((groups - 1,) + tile, jnp.float32),
            pltpu.VMEM(tile, jnp.float32),
            pltpu.VMEM((n - 1,) + tile, jnp.float32),
            dma((2,)),
            dma(()), dma(()),
            dma((2,)), dma((2,)),
            dma(()), dma((halves,)),
            dma(()), dma((halves, all_rows // BLOCK)),
            dma(()), dma(()),
            dma(()), dma(()),
            dma(()), dma(()),
        ],
        compiler_params=pltpu.CompilerParams(
            collective_id=0, has_side_effects=True, vmem_limit_bytes=32 << 20
        ),
    )(*[hbm(x) for x in (gradient, first_moment, second_moment, basis)], step_number, matrix_ids)
    return place(results)


def solution(mesh):
    in_specs = (
        P("group", "fsdp", None),
        P("group", "fsdp", None),
        P("group", "fsdp", None),
        P("group", "fsdp", None),
        P(),
        P("group"),
    )
    out_specs = (P("group", "fsdp", None), P("group", "fsdp", None), P("group", "fsdp", None))
    return jax.shard_map(local, mesh=mesh, in_specs=in_specs, out_specs=out_specs, check_vma=False)
```

```python
import functools
import math

import jax
import jax.numpy as jnp
from jax import lax
from jax.experimental import pallas as pl
from jax.experimental.pallas import tpu as pltpu
from jax.sharding import PartitionSpec as P

BLOCK = 256


BETA_ONE = 0.95
BETA_TWO = 0.95
ADAM_EPS = 1e-08
HIGHEST = lax.Precision.HIGHEST


def clip_of(local_squares, entries):
    total = lax.psum(local_squares, ("fsdp", "group"))
    return jnp.float32(math.sqrt(entries)) / (jnp.sqrt(total) + 1e-06)


def local_general(gradient, first_moment, second_moment, basis_store, step_number, matrix_ids):
    fsdp_count = lax.axis_size("fsdp")
    group_count = lax.axis_size("group")
    row_count = gradient.shape[1]
    col_count = gradient.shape[2]
    all_rows = row_count * fsdp_count
    col_share = col_count // fsdp_count
    left_blocks = all_rows // BLOCK
    right_blocks = col_count // BLOCK
    entries = all_rows * col_count * group_count
    grad_local = gradient[0].astype(jnp.float32)
    local_squares = jnp.sum(grad_local * grad_local)
    gathered = lax.all_gather(basis_store[0], "fsdp", axis=0, tiled=True)
    owner_rows = basis_store.shape[1]
    owner = (step_number[0] + matrix_ids[0]) % fsdp_count
    ordered_half = jnp.roll(gathered, -owner * owner_rows, axis=0)
    left = ordered_half[:all_rows].astype(jnp.float32).reshape(left_blocks, BLOCK, BLOCK)
    right_half = ordered_half[all_rows:].reshape(right_blocks, BLOCK, BLOCK)
    right = right_half.astype(jnp.float32)
    turned = jnp.einsum(
        "rbj,bjl->rbl",
        gradient[0].reshape(row_count, right_blocks, BLOCK),
        right_half,
        preferred_element_type=jnp.float32,
    )
    turned = clip_of(local_squares, entries) * turned
    outgoing = turned.reshape(row_count, fsdp_count, col_share)
    received = lax.all_to_all(outgoing, "fsdp", split_axis=1, concat_axis=0, tiled=True)
    width = received.shape[2]
    columns = received[:, 0, :].reshape(left_blocks, BLOCK, width)
    rotated = jnp.einsum("bkc,bki->cbi", columns, left, precision=HIGHEST).reshape(width, all_rows)
    count = step_number[0].astype(jnp.float32)
    first_fix = 1.0 - jnp.power(jnp.float32(BETA_ONE), count)
    second_fix = 1.0 - jnp.power(jnp.float32(BETA_TWO), count)
    first_sum = BETA_ONE * first_moment[0].astype(jnp.float32) + (1.0 - BETA_ONE) * rotated
    second_sum = (
        BETA_TWO * second_moment[0].astype(jnp.float32) + (1.0 - BETA_TWO) * rotated * rotated
    )
    direction = first_sum / first_fix / (jnp.sqrt(second_sum / second_fix) + ADAM_EPS)
    backward = jnp.einsum(
        "cbi,bki->cbk", direction.reshape(col_share, left_blocks, BLOCK), left, precision=HIGHEST
    )
    returning = backward.reshape(col_share, fsdp_count, row_count)
    received = lax.all_to_all(returning, "fsdp", split_axis=1, concat_axis=0, tiled=True)
    width = received.shape[2]
    pieces = received[:, 0, :].reshape(right_blocks, BLOCK, width)
    result = jnp.einsum("blr,bjl->rbj", pieces, right, precision=HIGHEST).reshape(width, col_count)
    return (
        result[None].astype(jnp.bfloat16),
        first_sum[None].astype(jnp.bfloat16),
        second_sum[None].astype(jnp.bfloat16),
    )


SLAB = 16
LANES = 128
PARTS = 1
LEAD = 1
MESH = pl.DeviceIdType.MESH


def pieces_of(x):
    high = x.astype(jnp.bfloat16)
    rest = x - high.astype(jnp.float32)
    middle = rest.astype(jnp.bfloat16)
    low = (rest - middle.astype(jnp.float32)).astype(jnp.bfloat16)
    return high, middle, low


def mm(a, b, dims):
    return lax.dot_general(a, b, (dims, ((), ())), preferred_element_type=jnp.float32)


NN = ((1,), (0,))
NT = ((1,), (1,))


def kernel(n, groups, grad, first, second, basis, step, ident, out_u, out_1, out_2,
           own, moments, hop, staged, left, right, got, upd, sq_own, sq_f, sq_mid, sq_z, sq_all,
           loc, hop_s, hop_r, left_s, left_r, right_s, right_r, got_s, got_r,
           ret_s, ret_r, f_s, f_r, z_s, z_r, t_s, t_r, ack):
    me = lax.axis_index("fsdp")
    zz = lax.axis_index("group")
    share = grad.shape[1]
    cols = grad.shape[2]
    width = cols // n
    halves = width // BLOCK
    slabs = n // 2
    per_owner = basis.shape[0]
    span = slabs * SLAB
    left_groups = left.shape[0]
    all_rows = share * n
    left_blocks = all_rows // BLOCK
    block_groups = BLOCK // span
    entries = float(share * n * cols * groups)

    core = lax.rem(me, 2)
    per = n // left_blocks
    masks = [m for m in range(2, n, 2)] + [m for m in range(3, n, 2)]
    swapped = [masks[i + 1] if i % 2 == 0 and i + 1 < len(masks) else masks[i - i % 2] for i in range(len(masks))]
    order = list(zip(masks, swapped)) + [(1, 1)]

    def peer(m):
        other = me
        for bit in (1 << i for i in range(n.bit_length() - 1)):
            if m & bit:
                other = other + bit * (1 - 2 * lax.rem(me // bit, 2))
        return other

    def pick(pair):
        a, b = pair
        return a + core * (b - a), peer(a) + core * (peer(b) - peer(a))

    def zpeer(k):
        return lax.rem(zz + k, groups)

    def lanes_of(c):
        return pl.ds(pl.multiple_of(lax.rem(c, 2) * LANES, LANES), LANES)

    def rows_of(c):
        return pl.ds(pl.multiple_of((c // 2) * SLAB, SLAB), SLAB)

    def share_rows(d):
        return pl.ds(pl.multiple_of(d * share, share), share)

    def out_cols(d, t):
        return pl.ds(pl.multiple_of(d * width + t * BLOCK, BLOCK), BLOCK)

    def settle(ref, sem):
        pltpu.make_async_copy(ref, ref, sem).wait()

    def remote(src, dst, ssem, rsem, d):
        return pltpu.make_async_remote_copy(
            src_ref=src, dst_ref=dst, send_sem=ssem, recv_sem=rsem,
            device_id={"fsdp": d}, device_id_type=MESH)

    locals_ = [
        pltpu.make_async_copy(grad.at[0], own, loc.at[0]),
        pltpu.make_async_copy(basis.at[:, me // 2, :, lanes_of(me)], hop.at[me], hop_r),
        pltpu.make_async_copy(first.at[0], moments.at[0], loc.at[1]),
        pltpu.make_async_copy(second.at[0], moments.at[1], loc.at[1]),
    ]
    for t in range(halves):
        locals_.append(pltpu.make_async_copy(
            grad.at[0, :, out_cols(me, t)], got.at[t, share_rows(me)], got_r.at[t, 0]))
    for copy in locals_:
        copy.start()

    leads = me == LEAD
    follows = me != LEAD
    barrier = pltpu.get_barrier_semaphore()
    for f in range(n):
        if f != LEAD:
            @pl.when(me != f)
            def _():
                pl.semaphore_signal(barrier, inc=1, device_id={"fsdp": f}, device_id_type=MESH)

    @pl.when(leads)
    def _():
        for k in range(1, groups):
            pl.semaphore_signal(barrier, inc=1, device_id={"group": zpeer(k)}, device_id_type=MESH)

    @pl.when(follows)
    def _():
        pl.semaphore_wait(barrier, n - 1)
        pl.semaphore_signal(ack, inc=1, device_id={"fsdp": LEAD}, device_id_type=MESH)

    @pl.when(leads)
    def _():
        pl.semaphore_wait(ack, n - 1)

    def hop_copy(m, d):
        return remote(basis.at[:, d // 2, :, lanes_of(d)], hop.at[me], hop_s, hop_r, d)

    def got_copy(t, m, d):
        return remote(own.at[:, out_cols(d, t)], got.at[t, share_rows(me)],
                      got_s, got_r.at[t, m // per], d)

    def right_copy(t, m, d):
        src = staged.at[pl.ds(left_groups + (d * halves + t) * block_groups, block_groups)]
        dst = right.at[t, :, rows_of(me), lanes_of(me)]
        return remote(src, dst, right_s, right_r.at[t], d)

    def left_copy(m, d):
        return remote(staged.at[pl.ds(0, left_groups)], left.at[:, rows_of(me), lanes_of(me)],
                      left_s.at[0], left_r.at[0], d)

    for pair in order:
        hop_copy(*pick(pair)).start()
    shared = left.at[:, :, lanes_of(me)]
    sibling = remote(shared, shared, left_s.at[1], left_r.at[1], peer(1))

    def send_got(t):
        for pair in order:
            got_copy(t, *pick(pair)).start()

    locals_[0].wait()
    squares = jnp.zeros((8, LANES), jnp.float32)
    for r in range(0, share, 16):
        rows = own[r:r + 16, :].astype(jnp.float32)
        rows = rows * rows
        rows = rows[0:8] + rows[8:16]
        for c in range(0, cols, LANES):
            squares = squares + rows[:, c:c + LANES]
    sq_own[...] = squares

    @pl.when(follows)
    def _():
        remote(sq_own, sq_f.at[lax.rem(me + n - LEAD - 1, n)], f_s, f_r, LEAD).start()

    send_got(0)

    @pl.when(leads)
    def _():
        settle(sq_f, f_r)
        squares = sq_own[...]
        for k in range(n - 1):
            squares = squares + sq_f[k]
        sq_mid[...] = squares
        pl.semaphore_wait(barrier, groups - 1)
        for k in range(1, groups):
            pltpu.make_async_remote_copy(
                src_ref=sq_mid, dst_ref=sq_z.at[k - 1], send_sem=z_s, recv_sem=z_r,
                device_id={"group": zpeer(k)}, device_id_type=MESH).start()

    settle(hop, hop_r)
    owner = lax.rem(step[0] + ident[0], n)
    for q in range(n):
        staged[q * per_owner:(q + 1) * per_owner] = hop[lax.rem(owner + q, n)]

    own_left = pltpu.make_async_copy(
        staged.at[pl.ds(0, left_groups)], left.at[:, rows_of(me), lanes_of(me)], left_r.at[0])
    own_left.start()
    for t in range(halves):
        pltpu.make_async_copy(
            staged.at[pl.ds(left_groups + (me * halves + t) * block_groups, block_groups)],
            right.at[t, :, rows_of(me), lanes_of(me)], right_r.at[t]).start()
    lefts_order = [m for m in order if m[0] % 2 == 0]
    def send_right(t):
        for pair in order:
            right_copy(t, *pick(pair)).start()

    send_right(0)
    for m, _ in lefts_order:
        left_copy(m, peer(m)).start()

    @pl.when(leads)
    def _():
        settle(sq_z, z_r)
        squares = sq_mid[...]
        for k in range(groups - 1):
            squares = squares + sq_z[k]
        sq_all[...] = squares
        for f in range(n):
            if f != LEAD:
                remote(sq_all, sq_all, t_s, t_r, f).start()

    for t in range(1, halves):
        send_right(t)
        send_got(t)

    count = jnp.full((1, 1), step[0].astype(jnp.float32))
    first_inv = 1.0 / (1.0 - jnp.exp(count * jnp.float32(math.log(BETA_ONE))))
    second_inv = 1.0 / (1.0 - jnp.exp(count * jnp.float32(math.log(BETA_TWO))))

    settle(shared, left_r.at[0])
    sibling.start()
    clip = None
    for t in range(halves):
        settle(right.at[t], right_r.at[t])
        rt = right[t].reshape(BLOCK, BLOCK)
        flipped = rt.astype(jnp.float32).T.astype(jnp.bfloat16)
        cut = slice(t * BLOCK, (t + 1) * BLOCK)
        if t == 0:
            sibling.wait_recv()
        for i in reversed(range(left_blocks)):
            b = peer(i * per) // per
            cols_b = pl.ds(pl.multiple_of(b * BLOCK, BLOCK), BLOCK)
            near = range(i * per, (i + 1) * per)
            settle(got.at[t, cols_b], got_r.at[t, i])
            lb = left[pl.ds(b * block_groups, block_groups)].reshape(BLOCK, BLOCK)
            turned = mm(flipped, got[t, cols_b, :], NT)
            rotated = sum(mm(piece, lb, NN) for piece in pieces_of(turned))
            if clip is None:
                @pl.when(follows)
                def _():
                    settle(sq_all, t_r)

                total = jnp.sum(sq_all[...], keepdims=True)
                clip = jnp.float32(math.sqrt(entries)) / (jnp.sqrt(total) + 1e-06)
                settle(moments, loc.at[1])

            rotated = rotated * clip
            first_sum = BETA_ONE * moments[0, cut, cols_b].astype(jnp.float32) + (1.0 - BETA_ONE) * rotated
            second_sum = (BETA_TWO * moments[1, cut, cols_b].astype(jnp.float32)
                          + (1.0 - BETA_TWO) * rotated * rotated)
            out_1[0, cut, cols_b] = first_sum.astype(jnp.bfloat16)
            out_2[0, cut, cols_b] = second_sum.astype(jnp.bfloat16)
            direction = first_sum * first_inv / (jnp.sqrt(second_sum * second_inv) + ADAM_EPS)
            back = sum(mm(rt, piece, NN) for piece in pieces_of(direction))
            result = sum(mm(lb, piece, NT) for piece in pieces_of(back))
            upd[t, cols_b, :] = result.astype(jnp.bfloat16)
            for m in reversed(near):
                src = upd.at[t, share_rows(peer(m))]
                dst = out_u.at[0, :, out_cols(me, t)]
                if m == 0:
                    copy = pltpu.make_async_copy(src, dst, ret_r)
                else:
                    copy = remote(src, dst, ret_s, ret_r, peer(m))
                copy.start()

    settle(hop.at[pl.ds(0, n - 1)], hop_s)

    @pl.when(follows)
    def _():
        settle(sq_own, f_s)

    @pl.when(leads)
    def _():
        settle(sq_z, z_s)
        settle(sq_f, t_s)

    settle(staged.at[pl.ds(0, (n // 2 - 1) * left_groups)], left_s.at[0])
    sibling.wait_send()
    settle(staged.at[pl.ds(0, (n - 1) * halves * block_groups)], right_s)
    settle(got.at[:, pl.ds(0, all_rows - share)], got_s)
    settle(upd.at[:, pl.ds(0, all_rows - share)], ret_s)
    settle(out_u, ret_r)


def hbm(x):
    return pltpu.with_memory_space_constraint(x, pltpu.MemorySpace.HBM)


def copy_kernel(a, b, c, x, y, z, sems):
    copies = []
    for src, dst in ((a, x), (b, y), (c, z)):
        rows = src.shape[1] // PARTS
        for i in range(PARTS):
            cut = pl.ds(i * rows, rows)
            copies.append(pltpu.make_async_copy(
                src.at[0, cut], dst.at[0, cut], sems.at[len(copies)]))
    for copy in copies:
        copy.start()
    for copy in copies:
        copy.wait()


def place(arrays):
    return pl.pallas_call(
        copy_kernel,
        out_shape=tuple(jax.ShapeDtypeStruct(a.shape, a.dtype) for a in arrays),
        in_specs=[pl.BlockSpec(memory_space=pltpu.VMEM)] * 3,
        out_specs=(pl.BlockSpec(memory_space=pl.ANY),) * 3,
        scratch_shapes=[pltpu.SemaphoreType.DMA((3 * PARTS,))],
        compiler_params=pltpu.CompilerParams(vmem_limit_bytes=8 << 20),
    )(*arrays)


def fits(gradient, first_moment, basis_store, n):
    if n < 2 or n & (n - 1):
        return False
    span = n // 2 * SLAB
    width = gradient.shape[2] // n
    all_rows = gradient.shape[1] * n
    return (
        BLOCK % span == 0
        and basis_store.shape[1] % span == 0
        and width % BLOCK == 0
        and all_rows % BLOCK == 0
        and n % (all_rows // BLOCK) == 0
        and gradient.shape[1] % SLAB == 0
        and all_rows <= 1024
        and width <= 1024
    )


def local(gradient, first_moment, second_moment, basis_store, step_number, matrix_ids):
    n = lax.axis_size("fsdp")
    groups = lax.axis_size("group")
    if not fits(gradient, first_moment, basis_store, n):
        return local_general(
            gradient, first_moment, second_moment, basis_store, step_number, matrix_ids
        )
    share, cols = gradient.shape[1:]
    all_rows = share * n
    width = cols // n
    halves = width // BLOCK
    slabs = n // 2
    span = slabs * SLAB
    per_owner = basis_store.shape[1] // span
    basis = basis_store.reshape(per_owner, slabs, SLAB, BLOCK)
    half = jnp.bfloat16
    anywhere = pl.BlockSpec(memory_space=pl.ANY)
    scalar = pl.BlockSpec(memory_space=pltpu.SMEM)
    dma = pltpu.SemaphoreType.DMA
    tile = (8, LANES)
    results = pl.pallas_call(
        functools.partial(kernel, n, groups),
        out_shape=(
            jax.ShapeDtypeStruct(gradient.shape, half),
            jax.ShapeDtypeStruct(first_moment.shape, half),
            jax.ShapeDtypeStruct(second_moment.shape, half),
        ),
        in_specs=[anywhere] * 4 + [scalar] * 2,
        out_specs=(pl.BlockSpec(memory_space=pltpu.VMEM),) * 3,
        scratch_shapes=[
            pltpu.VMEM((share, cols), half),
            pltpu.VMEM((2, width, all_rows), half),
            pltpu.VMEM((n, per_owner, SLAB, LANES), half),
            pltpu.VMEM((n * per_owner, SLAB, LANES), half),
            pltpu.VMEM((all_rows // span, span, BLOCK), half),
            pltpu.VMEM((halves, BLOCK // span, span, BLOCK), half),
            pltpu.VMEM((halves, all_rows, BLOCK), half),
            pltpu.VMEM((halves, all_rows, BLOCK), half),
            pltpu.VMEM(tile, jnp.float32),
            pltpu.VMEM((n - 1,) + tile, jnp.float32),
            pltpu.VMEM(tile, jnp.float32),
            pltpu.VMEM((groups - 1,) + tile, jnp.float32),
            pltpu.VMEM(tile, jnp.float32),
            dma((2,)),
            dma(()), dma(()),
            dma((2,)), dma((2,)),
            dma(()), dma((halves,)),
            dma(()), dma((halves, all_rows // BLOCK)),
            dma(()), dma(()),
            dma(()), dma(()),
            dma(()), dma(()),
            dma(()), dma(()),
            pltpu.SemaphoreType.REGULAR,
        ],
        compiler_params=pltpu.CompilerParams(
            collective_id=0, has_side_effects=True, vmem_limit_bytes=32 << 20
        ),
    )(*[hbm(x) for x in (gradient, first_moment, second_moment, basis)], step_number, matrix_ids)
    return place(results)


def solution(mesh):
    in_specs = (
        P("group", "fsdp", None),
        P("group", "fsdp", None),
        P("group", "fsdp", None),
        P("group", "fsdp", None),
        P(),
        P("group"),
    )
    out_specs = (P("group", "fsdp", None), P("group", "fsdp", None), P("group", "fsdp", None))
    return jax.shard_map(local, mesh=mesh, in_specs=in_specs, out_specs=out_specs, check_vma=False)
```

```python
import functools
import math

import jax
import jax.numpy as jnp
from jax import lax
from jax.experimental import pallas as pl
from jax.experimental.pallas import tpu as pltpu
from jax.sharding import PartitionSpec as P

BLOCK = 256


BETA_ONE = 0.95
BETA_TWO = 0.95
ADAM_EPS = 1e-08
HIGHEST = lax.Precision.HIGHEST


def clip_of(local_squares, entries):
    total = lax.psum(local_squares, ("fsdp", "group"))
    return jnp.float32(math.sqrt(entries)) / (jnp.sqrt(total) + 1e-06)


def local_general(gradient, first_moment, second_moment, basis_store, step_number, matrix_ids):
    fsdp_count = lax.axis_size("fsdp")
    group_count = lax.axis_size("group")
    row_count = gradient.shape[1]
    col_count = gradient.shape[2]
    all_rows = row_count * fsdp_count
    col_share = col_count // fsdp_count
    left_blocks = all_rows // BLOCK
    right_blocks = col_count // BLOCK
    entries = all_rows * col_count * group_count
    grad_local = gradient[0].astype(jnp.float32)
    local_squares = jnp.sum(grad_local * grad_local)
    gathered = lax.all_gather(basis_store[0], "fsdp", axis=0, tiled=True)
    owner_rows = basis_store.shape[1]
    owner = (step_number[0] + matrix_ids[0]) % fsdp_count
    ordered_half = jnp.roll(gathered, -owner * owner_rows, axis=0)
    left = ordered_half[:all_rows].astype(jnp.float32).reshape(left_blocks, BLOCK, BLOCK)
    right_half = ordered_half[all_rows:].reshape(right_blocks, BLOCK, BLOCK)
    right = right_half.astype(jnp.float32)
    turned = jnp.einsum(
        "rbj,bjl->rbl",
        gradient[0].reshape(row_count, right_blocks, BLOCK),
        right_half,
        preferred_element_type=jnp.float32,
    )
    turned = clip_of(local_squares, entries) * turned
    outgoing = turned.reshape(row_count, fsdp_count, col_share)
    received = lax.all_to_all(outgoing, "fsdp", split_axis=1, concat_axis=0, tiled=True)
    width = received.shape[2]
    columns = received[:, 0, :].reshape(left_blocks, BLOCK, width)
    rotated = jnp.einsum("bkc,bki->cbi", columns, left, precision=HIGHEST).reshape(width, all_rows)
    count = step_number[0].astype(jnp.float32)
    first_fix = 1.0 - jnp.power(jnp.float32(BETA_ONE), count)
    second_fix = 1.0 - jnp.power(jnp.float32(BETA_TWO), count)
    first_sum = BETA_ONE * first_moment[0].astype(jnp.float32) + (1.0 - BETA_ONE) * rotated
    second_sum = (
        BETA_TWO * second_moment[0].astype(jnp.float32) + (1.0 - BETA_TWO) * rotated * rotated
    )
    direction = first_sum / first_fix / (jnp.sqrt(second_sum / second_fix) + ADAM_EPS)
    backward = jnp.einsum(
        "cbi,bki->cbk", direction.reshape(col_share, left_blocks, BLOCK), left, precision=HIGHEST
    )
    returning = backward.reshape(col_share, fsdp_count, row_count)
    received = lax.all_to_all(returning, "fsdp", split_axis=1, concat_axis=0, tiled=True)
    width = received.shape[2]
    pieces = received[:, 0, :].reshape(right_blocks, BLOCK, width)
    result = jnp.einsum("blr,bjl->rbj", pieces, right, precision=HIGHEST).reshape(width, col_count)
    return (
        result[None].astype(jnp.bfloat16),
        first_sum[None].astype(jnp.bfloat16),
        second_sum[None].astype(jnp.bfloat16),
    )


SLAB = 16
LANES = 128
PARTS = 1
LEAD = 1
MESH = pl.DeviceIdType.MESH


def pieces_of(x):
    high = x.astype(jnp.bfloat16)
    rest = x - high.astype(jnp.float32)
    middle = rest.astype(jnp.bfloat16)
    low = (rest - middle.astype(jnp.float32)).astype(jnp.bfloat16)
    return high, middle, low


def mm(a, b, dims):
    return lax.dot_general(a, b, (dims, ((), ())), preferred_element_type=jnp.float32)


NN = ((1,), (0,))
NT = ((1,), (1,))


def kernel(n, groups, grad, first, second, basis, step, ident, out_u, out_1, out_2,
           held, own, moments, hop, staged, left, right, got, upd, sq_own, sq_f, sq_mid, sq_z, sq_all,
           loc, hop_s, hop_r, left_s, left_r, right_s, right_r, got_s, got_r,
           ret_s, ret_r, f_s, f_r, z_s, z_r, t_s, t_r):
    me = lax.axis_index("fsdp")
    zz = lax.axis_index("group")
    share = grad.shape[1]
    cols = grad.shape[2]
    width = cols // n
    halves = width // BLOCK
    slabs = n // 2
    per_owner = basis.shape[0]
    span = slabs * SLAB
    left_groups = left.shape[0]
    all_rows = share * n
    left_blocks = all_rows // BLOCK
    block_groups = BLOCK // span
    entries = float(share * n * cols * groups)

    core = lax.rem(me, 2)
    per = n // left_blocks
    masks = [m for m in range(2, n, 2)] + [m for m in range(3, n, 2)]
    swapped = [masks[i + 1] if i % 2 == 0 and i + 1 < len(masks) else masks[i - i % 2] for i in range(len(masks))]
    order = list(zip(masks, swapped)) + [(1, 1)]

    def peer(m):
        other = me
        for bit in (1 << i for i in range(n.bit_length() - 1)):
            if m & bit:
                other = other + bit * (1 - 2 * lax.rem(me // bit, 2))
        return other

    def pick(pair):
        a, b = pair
        return a + core * (b - a), peer(a) + core * (peer(b) - peer(a))

    def lanes_of(c):
        return pl.ds(pl.multiple_of(lax.rem(c, 2) * LANES, LANES), LANES)

    def rows_of(c):
        return pl.ds(pl.multiple_of((c // 2) * SLAB, SLAB), SLAB)

    def share_rows(d):
        return pl.ds(pl.multiple_of(d * share, share), share)

    def out_cols(d, t):
        return pl.ds(pl.multiple_of(d * width + t * BLOCK, BLOCK), BLOCK)

    def settle(ref, sem):
        pltpu.make_async_copy(ref, ref, sem).wait()

    def remote(src, dst, ssem, rsem, d):
        return pltpu.make_async_remote_copy(
            src_ref=src, dst_ref=dst, send_sem=ssem, recv_sem=rsem,
            device_id={"fsdp": d}, device_id_type=MESH)

    def across(src, dst, g):
        return pltpu.make_async_remote_copy(
            src_ref=src, dst_ref=dst, send_sem=z_s, recv_sem=z_r,
            device_id={"group": g}, device_id_type=MESH)

    locals_ = [
        pltpu.make_async_copy(grad.at[0], own, loc.at[0]),
        pltpu.make_async_copy(basis, held, loc.at[2]),
        pltpu.make_async_copy(first.at[0], moments.at[0], loc.at[1]),
        pltpu.make_async_copy(second.at[0], moments.at[1], loc.at[1]),
    ]
    for t in range(halves):
        locals_.append(pltpu.make_async_copy(
            grad.at[0, :, out_cols(me, t)], got.at[t, share_rows(me)], got_r.at[t, 0]))
    leads = me == LEAD
    follows = me != LEAD
    roots = jnp.logical_and(leads, zz == 0)
    relays = jnp.logical_and(leads, zz != 0)
    barrier = pltpu.get_barrier_semaphore()
    for k in range(1, n):
        pl.semaphore_signal(barrier, inc=1, device_id={"fsdp": peer(k)}, device_id_type=MESH)

    @pl.when(roots)
    def _():
        for g in range(1, groups):
            pl.semaphore_signal(barrier, inc=1, device_id={"group": g}, device_id_type=MESH)

    for copy in (locals_[1], locals_[0]):
        copy.start()

    @pl.when(relays)
    def _():
        pl.semaphore_wait(barrier, n)

    @pl.when(jnp.logical_not(relays))
    def _():
        pl.semaphore_wait(barrier, n - 1)

    def hop_copy(m, d):
        return remote(held.at[:, d // 2, :, lanes_of(d)], hop.at[me], hop_s, hop_r, d)

    def got_copy(t, m, d):
        return remote(own.at[:, out_cols(d, t)], got.at[t, share_rows(me)],
                      got_s, got_r.at[t, m // per], d)

    def right_copy(t, m, d):
        src = staged.at[pl.ds(left_groups + (d * halves + t) * block_groups, block_groups)]
        dst = right.at[t, :, rows_of(me), lanes_of(me)]
        return remote(src, dst, right_s, right_r.at[t], d)

    def left_copy(m, d):
        return remote(staged.at[pl.ds(0, left_groups)], left.at[:, rows_of(me), lanes_of(me)],
                      left_s.at[0], left_r.at[0], d)

    locals_[1].wait()
    for pair in order:
        hop_copy(*pick(pair)).start()
    pltpu.make_async_copy(held.at[:, me // 2, :, lanes_of(me)], hop.at[me], hop_r).start()
    for copy in locals_[2:]:
        copy.start()
    shared = left.at[:, :, lanes_of(me)]
    sibling = remote(shared, shared, left_s.at[1], left_r.at[1], peer(1))

    def send_got(t):
        for pair in order:
            got_copy(t, *pick(pair)).start()

    locals_[0].wait()
    squares = jnp.zeros((8, LANES), jnp.float32)
    for r in range(0, share, 16):
        rows = own[r:r + 16, :].astype(jnp.float32)
        rows = rows * rows
        rows = rows[0:8] + rows[8:16]
        for c in range(0, cols, LANES):
            squares = squares + rows[:, c:c + LANES]
    sq_own[...] = squares

    @pl.when(follows)
    def _():
        remote(sq_own, sq_f.at[lax.rem(me + n - LEAD - 1, n)], f_s, f_r, LEAD).start()

    send_got(0)

    @pl.when(leads)
    def _():
        settle(sq_f, f_r)
        squares = sq_own[...]
        for k in range(n - 1):
            squares = squares + sq_f[k]
        sq_mid[...] = squares

    @pl.when(relays)
    def _():
        across(sq_mid, sq_z.at[lax.rem(zz + groups - 1, groups)], 0).start()

    settle(hop, hop_r)
    owner = lax.rem(step[0] + ident[0], n)
    for q in range(n):
        staged[q * per_owner:(q + 1) * per_owner] = hop[lax.rem(owner + q, n)]

    own_left = pltpu.make_async_copy(
        staged.at[pl.ds(0, left_groups)], left.at[:, rows_of(me), lanes_of(me)], left_r.at[0])
    own_left.start()
    for t in range(halves):
        pltpu.make_async_copy(
            staged.at[pl.ds(left_groups + (me * halves + t) * block_groups, block_groups)],
            right.at[t, :, rows_of(me), lanes_of(me)], right_r.at[t]).start()
    lefts_order = [m for m in order if m[0] % 2 == 0]
    def send_right(t):
        for pair in order:
            right_copy(t, *pick(pair)).start()

    send_right(0)
    for m, _ in lefts_order:
        left_copy(m, peer(m)).start()

    @pl.when(roots)
    def _():
        settle(sq_z, z_r)
        squares = sq_mid[...]
        for k in range(groups - 1):
            squares = squares + sq_z[k]
        sq_all[...] = squares
        for g in range(1, groups):
            across(sq_all, sq_all, g).start()

    @pl.when(relays)
    def _():
        settle(sq_all, z_r)

    @pl.when(leads)
    def _():
        for f in range(n):
            if f != LEAD:
                remote(sq_all, sq_all, t_s, t_r, f).start()

    for t in range(1, halves):
        send_right(t)
        send_got(t)

    count = jnp.full((1, 1), step[0].astype(jnp.float32))
    first_inv = 1.0 / (1.0 - jnp.exp(count * jnp.float32(math.log(BETA_ONE))))
    second_inv = 1.0 / (1.0 - jnp.exp(count * jnp.float32(math.log(BETA_TWO))))

    settle(shared, left_r.at[0])
    sibling.start()
    clip = None
    for t in range(halves):
        settle(right.at[t], right_r.at[t])
        rt = right[t].reshape(BLOCK, BLOCK)
        flipped = rt.astype(jnp.float32).T.astype(jnp.bfloat16)
        cut = slice(t * BLOCK, (t + 1) * BLOCK)
        if t == 0:
            sibling.wait_recv()
        for i in reversed(range(left_blocks)):
            b = peer(i * per) // per
            cols_b = pl.ds(pl.multiple_of(b * BLOCK, BLOCK), BLOCK)
            near = range(i * per, (i + 1) * per)
            settle(got.at[t, cols_b], got_r.at[t, i])
            lb = left[pl.ds(b * block_groups, block_groups)].reshape(BLOCK, BLOCK)
            turned = mm(flipped, got[t, cols_b, :], NT)
            rotated = sum(mm(piece, lb, NN) for piece in pieces_of(turned))
            if clip is None:
                @pl.when(follows)
                def _():
                    settle(sq_all, t_r)

                total = jnp.sum(sq_all[...], keepdims=True)
                clip = jnp.float32(math.sqrt(entries)) / (jnp.sqrt(total) + 1e-06)
                settle(moments, loc.at[1])

            rotated = rotated * clip
            first_sum = BETA_ONE * moments[0, cut, cols_b].astype(jnp.float32) + (1.0 - BETA_ONE) * rotated
            second_sum = (BETA_TWO * moments[1, cut, cols_b].astype(jnp.float32)
                          + (1.0 - BETA_TWO) * rotated * rotated)
            out_1[0, cut, cols_b] = first_sum.astype(jnp.bfloat16)
            out_2[0, cut, cols_b] = second_sum.astype(jnp.bfloat16)
            direction = first_sum * first_inv / (jnp.sqrt(second_sum * second_inv) + ADAM_EPS)
            back = sum(mm(rt, piece, NN) for piece in pieces_of(direction))
            result = sum(mm(lb, piece, NT) for piece in pieces_of(back))
            upd[t, cols_b, :] = result.astype(jnp.bfloat16)
            for m in reversed(near):
                src = upd.at[t, share_rows(peer(m))]
                dst = out_u.at[0, :, out_cols(me, t)]
                if m == 0:
                    copy = pltpu.make_async_copy(src, dst, ret_r)
                else:
                    copy = remote(src, dst, ret_s, ret_r, peer(m))
                copy.start()

    settle(hop.at[pl.ds(0, n - 1)], hop_s)

    @pl.when(follows)
    def _():
        settle(sq_own, f_s)

    @pl.when(roots)
    def _():
        settle(sq_z, z_s)

    @pl.when(relays)
    def _():
        settle(sq_mid, z_s)

    @pl.when(leads)
    def _():
        settle(sq_f, t_s)

    settle(staged.at[pl.ds(0, (n // 2 - 1) * left_groups)], left_s.at[0])
    sibling.wait_send()
    settle(staged.at[pl.ds(0, (n - 1) * halves * block_groups)], right_s)
    settle(got.at[:, pl.ds(0, all_rows - share)], got_s)
    settle(upd.at[:, pl.ds(0, all_rows - share)], ret_s)
    settle(out_u, ret_r)


def hbm(x):
    return pltpu.with_memory_space_constraint(x, pltpu.MemorySpace.HBM)


def copy_kernel(a, b, c, x, y, z, sems):
    copies = []
    for src, dst in ((a, x), (b, y), (c, z)):
        rows = src.shape[1] // PARTS
        for i in range(PARTS):
            cut = pl.ds(i * rows, rows)
            copies.append(pltpu.make_async_copy(
                src.at[0, cut], dst.at[0, cut], sems.at[len(copies)]))
    for copy in copies:
        copy.start()
    for copy in copies:
        copy.wait()


def place(arrays):
    return pl.pallas_call(
        copy_kernel,
        out_shape=tuple(jax.ShapeDtypeStruct(a.shape, a.dtype) for a in arrays),
        in_specs=[pl.BlockSpec(memory_space=pltpu.VMEM)] * 3,
        out_specs=(pl.BlockSpec(memory_space=pl.ANY),) * 3,
        scratch_shapes=[pltpu.SemaphoreType.DMA((3 * PARTS,))],
        compiler_params=pltpu.CompilerParams(vmem_limit_bytes=8 << 20),
    )(*arrays)


def fits(gradient, first_moment, basis_store, n):
    if n < 2 or n & (n - 1):
        return False
    span = n // 2 * SLAB
    width = gradient.shape[2] // n
    all_rows = gradient.shape[1] * n
    return (
        BLOCK % span == 0
        and basis_store.shape[1] % span == 0
        and width % BLOCK == 0
        and all_rows % BLOCK == 0
        and n % (all_rows // BLOCK) == 0
        and gradient.shape[1] % SLAB == 0
        and all_rows <= 1024
        and width <= 1024
    )


def local(gradient, first_moment, second_moment, basis_store, step_number, matrix_ids):
    n = lax.axis_size("fsdp")
    groups = lax.axis_size("group")
    if not fits(gradient, first_moment, basis_store, n):
        return local_general(
            gradient, first_moment, second_moment, basis_store, step_number, matrix_ids
        )
    share, cols = gradient.shape[1:]
    all_rows = share * n
    width = cols // n
    halves = width // BLOCK
    slabs = n // 2
    span = slabs * SLAB
    per_owner = basis_store.shape[1] // span
    basis = basis_store.reshape(per_owner, slabs, SLAB, BLOCK)
    half = jnp.bfloat16
    anywhere = pl.BlockSpec(memory_space=pl.ANY)
    scalar = pl.BlockSpec(memory_space=pltpu.SMEM)
    dma = pltpu.SemaphoreType.DMA
    tile = (8, LANES)
    results = pl.pallas_call(
        functools.partial(kernel, n, groups),
        out_shape=(
            jax.ShapeDtypeStruct(gradient.shape, half),
            jax.ShapeDtypeStruct(first_moment.shape, half),
            jax.ShapeDtypeStruct(second_moment.shape, half),
        ),
        in_specs=[anywhere] * 4 + [scalar] * 2,
        out_specs=(pl.BlockSpec(memory_space=pltpu.VMEM),) * 3,
        scratch_shapes=[
            pltpu.VMEM(basis.shape, half),
            pltpu.VMEM((share, cols), half),
            pltpu.VMEM((2, width, all_rows), half),
            pltpu.VMEM((n, per_owner, SLAB, LANES), half),
            pltpu.VMEM((n * per_owner, SLAB, LANES), half),
            pltpu.VMEM((all_rows // span, span, BLOCK), half),
            pltpu.VMEM((halves, BLOCK // span, span, BLOCK), half),
            pltpu.VMEM((halves, all_rows, BLOCK), half),
            pltpu.VMEM((halves, all_rows, BLOCK), half),
            pltpu.VMEM(tile, jnp.float32),
            pltpu.VMEM((n - 1,) + tile, jnp.float32),
            pltpu.VMEM(tile, jnp.float32),
            pltpu.VMEM((groups - 1,) + tile, jnp.float32),
            pltpu.VMEM(tile, jnp.float32),
            dma((3,)),
            dma(()), dma(()),
            dma((2,)), dma((2,)),
            dma(()), dma((halves,)),
            dma(()), dma((halves, all_rows // BLOCK)),
            dma(()), dma(()),
            dma(()), dma(()),
            dma(()), dma(()),
            dma(()), dma(()),
        ],
        compiler_params=pltpu.CompilerParams(
            collective_id=0, has_side_effects=True, vmem_limit_bytes=32 << 20
        ),
    )(*[hbm(x) for x in (gradient, first_moment, second_moment, basis)], step_number, matrix_ids)
    return place(results)


def solution(mesh):
    in_specs = (
        P("group", "fsdp", None),
        P("group", "fsdp", None),
        P("group", "fsdp", None),
        P("group", "fsdp", None),
        P(),
        P("group"),
    )
    out_specs = (P("group", "fsdp", None), P("group", "fsdp", None), P("group", "fsdp", None))
    return jax.shard_map(local, mesh=mesh, in_specs=in_specs, out_specs=out_specs, check_vma=False)
```

```python
import functools
import math

import jax
import jax.numpy as jnp
from jax import lax
from jax.experimental import pallas as pl
from jax.experimental.pallas import tpu as pltpu
from jax.sharding import PartitionSpec as P

BLOCK = 256


BETA_ONE = 0.95
BETA_TWO = 0.95
ADAM_EPS = 1e-08
HIGHEST = lax.Precision.HIGHEST


def clip_of(local_squares, entries):
    total = lax.psum(local_squares, ("fsdp", "group"))
    return jnp.float32(math.sqrt(entries)) / (jnp.sqrt(total) + 1e-06)


def local_general(gradient, first_moment, second_moment, basis_store, step_number, matrix_ids):
    fsdp_count = lax.axis_size("fsdp")
    group_count = lax.axis_size("group")
    row_count = gradient.shape[1]
    col_count = gradient.shape[2]
    all_rows = row_count * fsdp_count
    col_share = col_count // fsdp_count
    left_blocks = all_rows // BLOCK
    right_blocks = col_count // BLOCK
    entries = all_rows * col_count * group_count
    grad_local = gradient[0].astype(jnp.float32)
    local_squares = jnp.sum(grad_local * grad_local)
    gathered = lax.all_gather(basis_store[0], "fsdp", axis=0, tiled=True)
    owner_rows = basis_store.shape[1]
    owner = (step_number[0] + matrix_ids[0]) % fsdp_count
    ordered_half = jnp.roll(gathered, -owner * owner_rows, axis=0)
    left = ordered_half[:all_rows].astype(jnp.float32).reshape(left_blocks, BLOCK, BLOCK)
    right_half = ordered_half[all_rows:].reshape(right_blocks, BLOCK, BLOCK)
    right = right_half.astype(jnp.float32)
    turned = jnp.einsum(
        "rbj,bjl->rbl",
        gradient[0].reshape(row_count, right_blocks, BLOCK),
        right_half,
        preferred_element_type=jnp.float32,
    )
    turned = clip_of(local_squares, entries) * turned
    outgoing = turned.reshape(row_count, fsdp_count, col_share)
    received = lax.all_to_all(outgoing, "fsdp", split_axis=1, concat_axis=0, tiled=True)
    width = received.shape[2]
    columns = received[:, 0, :].reshape(left_blocks, BLOCK, width)
    rotated = jnp.einsum("bkc,bki->cbi", columns, left, precision=HIGHEST).reshape(width, all_rows)
    count = step_number[0].astype(jnp.float32)
    first_fix = 1.0 - jnp.power(jnp.float32(BETA_ONE), count)
    second_fix = 1.0 - jnp.power(jnp.float32(BETA_TWO), count)
    first_sum = BETA_ONE * first_moment[0].astype(jnp.float32) + (1.0 - BETA_ONE) * rotated
    second_sum = (
        BETA_TWO * second_moment[0].astype(jnp.float32) + (1.0 - BETA_TWO) * rotated * rotated
    )
    direction = first_sum / first_fix / (jnp.sqrt(second_sum / second_fix) + ADAM_EPS)
    backward = jnp.einsum(
        "cbi,bki->cbk", direction.reshape(col_share, left_blocks, BLOCK), left, precision=HIGHEST
    )
    returning = backward.reshape(col_share, fsdp_count, row_count)
    received = lax.all_to_all(returning, "fsdp", split_axis=1, concat_axis=0, tiled=True)
    width = received.shape[2]
    pieces = received[:, 0, :].reshape(right_blocks, BLOCK, width)
    result = jnp.einsum("blr,bjl->rbj", pieces, right, precision=HIGHEST).reshape(width, col_count)
    return (
        result[None].astype(jnp.bfloat16),
        first_sum[None].astype(jnp.bfloat16),
        second_sum[None].astype(jnp.bfloat16),
    )


SLAB = 16
LANES = 128
PARTS = 1
LEAD = 1
MESH = pl.DeviceIdType.MESH


def pieces_of(x):
    high = x.astype(jnp.bfloat16)
    rest = x - high.astype(jnp.float32)
    middle = rest.astype(jnp.bfloat16)
    low = (rest - middle.astype(jnp.float32)).astype(jnp.bfloat16)
    return high, middle, low


def mm(a, b, dims):
    return lax.dot_general(a, b, (dims, ((), ())), preferred_element_type=jnp.float32)


NN = ((1,), (0,))
NT = ((1,), (1,))


def kernel(n, groups, grad, first, second, basis, step, ident, out_u, out_1, out_2,
           held, own, moments, hop, staged, left, right, got, upd, sq_own, sq_f, sq_mid, sq_z, sq_all,
           loc, hop_s, hop_r, left_s, left_r, right_s, right_r, got_s, got_r,
           ret_s, ret_r, f_s, f_r, z_s, z_r, t_s, t_r):
    me = lax.axis_index("fsdp")
    zz = lax.axis_index("group")
    share = grad.shape[1]
    cols = grad.shape[2]
    width = cols // n
    halves = width // BLOCK
    slabs = n // 2
    per_owner = basis.shape[0]
    span = slabs * SLAB
    left_groups = left.shape[0]
    all_rows = share * n
    left_blocks = all_rows // BLOCK
    block_groups = BLOCK // span
    entries = float(share * n * cols * groups)

    core = lax.rem(me, 2)
    per = n // left_blocks
    masks = [m for m in range(2, n, 2)] + [m for m in range(3, n, 2)]
    swapped = [masks[i + 1] if i % 2 == 0 and i + 1 < len(masks) else masks[i - i % 2] for i in range(len(masks))]
    order = list(zip(masks, swapped)) + [(1, 1)]

    def peer(m):
        other = me
        for bit in (1 << i for i in range(n.bit_length() - 1)):
            if m & bit:
                other = other + bit * (1 - 2 * lax.rem(me // bit, 2))
        return other

    def pick(pair):
        a, b = pair
        return a + core * (b - a), peer(a) + core * (peer(b) - peer(a))

    def lanes_of(c):
        return pl.ds(pl.multiple_of(lax.rem(c, 2) * LANES, LANES), LANES)

    def rows_of(c):
        return pl.ds(pl.multiple_of((c // 2) * SLAB, SLAB), SLAB)

    def share_rows(d):
        return pl.ds(pl.multiple_of(d * share, share), share)

    def out_cols(d, t):
        return pl.ds(pl.multiple_of(d * width + t * BLOCK, BLOCK), BLOCK)

    def settle(ref, sem):
        pltpu.make_async_copy(ref, ref, sem).wait()

    def remote(src, dst, ssem, rsem, d):
        return pltpu.make_async_remote_copy(
            src_ref=src, dst_ref=dst, send_sem=ssem, recv_sem=rsem,
            device_id={"fsdp": d}, device_id_type=MESH)

    def across(src, dst, g):
        return pltpu.make_async_remote_copy(
            src_ref=src, dst_ref=dst, send_sem=z_s, recv_sem=z_r,
            device_id={"group": g}, device_id_type=MESH)

    locals_ = [
        pltpu.make_async_copy(grad.at[0], own, loc.at[0]),
        pltpu.make_async_copy(basis, held, loc.at[2]),
        pltpu.make_async_copy(first.at[0], moments.at[0], loc.at[1]),
        pltpu.make_async_copy(second.at[0], moments.at[1], loc.at[1]),
    ]
    for t in range(halves):
        locals_.append(pltpu.make_async_copy(
            grad.at[0, :, out_cols(me, t)], got.at[t, share_rows(me)], got_r.at[t, 0]))
    leads = me == LEAD
    follows = me != LEAD
    roots = jnp.logical_and(leads, zz == 0)
    relays = jnp.logical_and(leads, zz != 0)
    barrier = pltpu.get_barrier_semaphore()
    for k in range(1, n):
        pl.semaphore_signal(barrier, inc=1, device_id={"fsdp": peer(k)}, device_id_type=MESH)

    @pl.when(roots)
    def _():
        for g in range(1, groups):
            pl.semaphore_signal(barrier, inc=1, device_id={"group": g}, device_id_type=MESH)

    for copy in (locals_[1], locals_[0]):
        copy.start()

    @pl.when(relays)
    def _():
        pl.semaphore_wait(barrier, n)

    @pl.when(jnp.logical_not(relays))
    def _():
        pl.semaphore_wait(barrier, n - 1)

    def hop_copy(m, d):
        return remote(held.at[:, d // 2, :, lanes_of(d)], hop.at[me], hop_s, hop_r, d)

    def got_copy(t, m, d):
        return remote(own.at[:, out_cols(d, t)], got.at[t, share_rows(me)],
                      got_s, got_r.at[t, m // per], d)

    def right_copy(t, m, d):
        src = staged.at[pl.ds(left_groups + (d * halves + t) * block_groups, block_groups)]
        dst = right.at[t, :, rows_of(me), lanes_of(me)]
        return remote(src, dst, right_s, right_r.at[t], d)

    def left_copy(m, d):
        return remote(staged.at[pl.ds(0, left_groups)], left.at[:, rows_of(me), lanes_of(me)],
                      left_s.at[0], left_r.at[0], d)

    locals_[1].wait()
    for pair in order:
        hop_copy(*pick(pair)).start()
    pltpu.make_async_copy(held.at[:, me // 2, :, lanes_of(me)], hop.at[me], hop_r).start()
    for copy in locals_[2:]:
        copy.start()
    shared = left.at[:, :, lanes_of(me)]
    sibling = remote(shared, shared, left_s.at[1], left_r.at[1], peer(1))

    def send_got(t, i=None):
        if i is None:
            pairs = order
        else:
            part = [m for m in masks if m // per == i]
            pairs = [(part[j], part[j + 1 - 2 * (j % 2)]) for j in range(len(part))]
            pairs = pairs + ([] if i else [(1, 1)])
        for pair in pairs:
            got_copy(t, *pick(pair)).start()

    locals_[0].wait()
    squares = jnp.zeros((8, LANES), jnp.float32)
    for r in range(0, share, 16):
        rows = own[r:r + 16, :].astype(jnp.float32)
        rows = rows * rows
        rows = rows[0:8] + rows[8:16]
        for c in range(0, cols, LANES):
            squares = squares + rows[:, c:c + LANES]
    sq_own[...] = squares

    @pl.when(follows)
    def _():
        remote(sq_own, sq_f.at[lax.rem(me + n - LEAD - 1, n)], f_s, f_r, LEAD).start()

    send_got(0)

    @pl.when(leads)
    def _():
        settle(sq_f, f_r)
        squares = sq_own[...]
        for k in range(n - 1):
            squares = squares + sq_f[k]
        sq_mid[...] = squares

    @pl.when(relays)
    def _():
        across(sq_mid, sq_z.at[lax.rem(zz + groups - 1, groups)], 0).start()

    settle(hop, hop_r)
    owner = lax.rem(step[0] + ident[0], n)
    left_shards = -(-left_groups // per_owner)

    def stage(q):
        staged[q * per_owner:(q + 1) * per_owner] = hop[lax.rem(owner + q, n)]

    def send_right(t):
        for pair in order:
            right_copy(t, *pick(pair)).start()

    for q in range(left_shards):
        stage(q)
    for m in [m for m in masks if m % 2 == 0]:
        left_copy(m, peer(m)).start()
    for q in range(left_shards, n):
        stage(q)
    send_right(0)
    pltpu.make_async_copy(
        staged.at[pl.ds(0, left_groups)], left.at[:, rows_of(me), lanes_of(me)],
        left_r.at[0]).start()
    for t in range(halves):
        pltpu.make_async_copy(
            staged.at[pl.ds(left_groups + (me * halves + t) * block_groups, block_groups)],
            right.at[t, :, rows_of(me), lanes_of(me)], right_r.at[t]).start()

    @pl.when(roots)
    def _():
        settle(sq_z, z_r)
        squares = sq_mid[...]
        for k in range(groups - 1):
            squares = squares + sq_z[k]
        sq_all[...] = squares
        for g in range(1, groups):
            across(sq_all, sq_all, g).start()

    @pl.when(relays)
    def _():
        settle(sq_all, z_r)

    @pl.when(leads)
    def _():
        for f in range(n):
            if f != LEAD:
                remote(sq_all, sq_all, t_s, t_r, f).start()

    send_got(1)
    send_right(1)

    count = jnp.full((1, 1), step[0].astype(jnp.float32))
    first_inv = 1.0 / (1.0 - jnp.exp(count * jnp.float32(math.log(BETA_ONE))))
    second_inv = 1.0 / (1.0 - jnp.exp(count * jnp.float32(math.log(BETA_TWO))))

    settle(shared, left_r.at[0])
    sibling.start()
    clip = None
    for t in range(halves):
        settle(right.at[t], right_r.at[t])
        rt = right[t].reshape(BLOCK, BLOCK)
        flipped = rt.astype(jnp.float32).T.astype(jnp.bfloat16)
        cut = slice(t * BLOCK, (t + 1) * BLOCK)
        if t == 0:
            sibling.wait_recv()
        for i in reversed(range(left_blocks)):
            b = peer(i * per) // per
            cols_b = pl.ds(pl.multiple_of(b * BLOCK, BLOCK), BLOCK)
            near = range(i * per, (i + 1) * per)
            settle(got.at[t, cols_b], got_r.at[t, i])
            lb = left[pl.ds(b * block_groups, block_groups)].reshape(BLOCK, BLOCK)
            turned = mm(flipped, got[t, cols_b, :], NT)
            rotated = sum(mm(piece, lb, NN) for piece in pieces_of(turned))
            if clip is None:
                @pl.when(follows)
                def _():
                    settle(sq_all, t_r)

                total = jnp.sum(sq_all[...], keepdims=True)
                clip = jnp.float32(math.sqrt(entries)) / (jnp.sqrt(total) + 1e-06)
                settle(moments, loc.at[1])

            rotated = rotated * clip
            first_sum = BETA_ONE * moments[0, cut, cols_b].astype(jnp.float32) + (1.0 - BETA_ONE) * rotated
            second_sum = (BETA_TWO * moments[1, cut, cols_b].astype(jnp.float32)
                          + (1.0 - BETA_TWO) * rotated * rotated)
            out_1[0, cut, cols_b] = first_sum.astype(jnp.bfloat16)
            out_2[0, cut, cols_b] = second_sum.astype(jnp.bfloat16)
            direction = first_sum * first_inv / (jnp.sqrt(second_sum * second_inv) + ADAM_EPS)
            back = sum(mm(rt, piece, NN) for piece in pieces_of(direction))
            result = sum(mm(lb, piece, NT) for piece in pieces_of(back))
            upd[t, cols_b, :] = result.astype(jnp.bfloat16)
            ahead = [m for m in reversed(near) if m > 1 and m % 2 == 0]
            swap = [m + 1 for m in ahead]
            for pair in list(zip(ahead[::-1], swap[::-1])) + list(zip(swap[::-1], ahead[::-1])) + ([] if i else [(1, 1)]):
                d = pick(pair)[1]
                remote(upd.at[t, share_rows(d)], out_u.at[0, :, out_cols(me, t)],
                       ret_s, ret_r, d).start()
            if i == 0:
                pltpu.make_async_copy(upd.at[t, share_rows(me)],
                                      out_u.at[0, :, out_cols(me, t)], ret_r).start()

    settle(hop.at[pl.ds(0, n - 1)], hop_s)

    @pl.when(follows)
    def _():
        settle(sq_own, f_s)

    @pl.when(roots)
    def _():
        settle(sq_z, z_s)

    @pl.when(relays)
    def _():
        settle(sq_mid, z_s)

    @pl.when(leads)
    def _():
        settle(sq_f, t_s)

    settle(staged.at[pl.ds(0, (n // 2 - 1) * left_groups)], left_s.at[0])
    sibling.wait_send()
    settle(staged.at[pl.ds(0, (n - 1) * halves * block_groups)], right_s)
    settle(got.at[:, pl.ds(0, all_rows - share)], got_s)
    settle(upd.at[:, pl.ds(0, all_rows - share)], ret_s)
    settle(out_u, ret_r)


def hbm(x):
    return pltpu.with_memory_space_constraint(x, pltpu.MemorySpace.HBM)


def copy_kernel(a, b, c, x, y, z, sems):
    copies = []
    for src, dst in ((a, x), (b, y), (c, z)):
        rows = src.shape[1] // PARTS
        for i in range(PARTS):
            cut = pl.ds(i * rows, rows)
            copies.append(pltpu.make_async_copy(
                src.at[0, cut], dst.at[0, cut], sems.at[len(copies)]))
    for copy in copies:
        copy.start()
    for copy in copies:
        copy.wait()


def place(arrays):
    return pl.pallas_call(
        copy_kernel,
        out_shape=tuple(jax.ShapeDtypeStruct(a.shape, a.dtype) for a in arrays),
        in_specs=[pl.BlockSpec(memory_space=pltpu.VMEM)] * 3,
        out_specs=(pl.BlockSpec(memory_space=pl.ANY),) * 3,
        scratch_shapes=[pltpu.SemaphoreType.DMA((3 * PARTS,))],
        compiler_params=pltpu.CompilerParams(vmem_limit_bytes=8 << 20),
    )(*arrays)


def fits(gradient, first_moment, basis_store, n):
    if n < 2 or n & (n - 1):
        return False
    span = n // 2 * SLAB
    width = gradient.shape[2] // n
    all_rows = gradient.shape[1] * n
    return (
        BLOCK % span == 0
        and basis_store.shape[1] % span == 0
        and width % BLOCK == 0
        and all_rows % BLOCK == 0
        and n % (all_rows // BLOCK) == 0
        and n // (all_rows // BLOCK) % 2 == 0
        and gradient.shape[1] % SLAB == 0
        and all_rows <= 1024
        and width <= 1024
    )


def local(gradient, first_moment, second_moment, basis_store, step_number, matrix_ids):
    n = lax.axis_size("fsdp")
    groups = lax.axis_size("group")
    if groups < 2 or not fits(gradient, first_moment, basis_store, n):
        return local_general(
            gradient, first_moment, second_moment, basis_store, step_number, matrix_ids
        )
    share, cols = gradient.shape[1:]
    all_rows = share * n
    width = cols // n
    halves = width // BLOCK
    slabs = n // 2
    span = slabs * SLAB
    per_owner = basis_store.shape[1] // span
    basis = basis_store.reshape(per_owner, slabs, SLAB, BLOCK)
    half = jnp.bfloat16
    anywhere = pl.BlockSpec(memory_space=pl.ANY)
    scalar = pl.BlockSpec(memory_space=pltpu.SMEM)
    dma = pltpu.SemaphoreType.DMA
    tile = (8, LANES)
    results = pl.pallas_call(
        functools.partial(kernel, n, groups),
        out_shape=(
            jax.ShapeDtypeStruct(gradient.shape, half),
            jax.ShapeDtypeStruct(first_moment.shape, half),
            jax.ShapeDtypeStruct(second_moment.shape, half),
        ),
        in_specs=[anywhere] * 4 + [scalar] * 2,
        out_specs=(pl.BlockSpec(memory_space=pltpu.VMEM),) * 3,
        scratch_shapes=[
            pltpu.VMEM(basis.shape, half),
            pltpu.VMEM((share, cols), half),
            pltpu.VMEM((2, width, all_rows), half),
            pltpu.VMEM((n, per_owner, SLAB, LANES), half),
            pltpu.VMEM((n * per_owner, SLAB, LANES), half),
            pltpu.VMEM((all_rows // span, span, BLOCK), half),
            pltpu.VMEM((halves, BLOCK // span, span, BLOCK), half),
            pltpu.VMEM((halves, all_rows, BLOCK), half),
            pltpu.VMEM((halves, all_rows, BLOCK), half),
            pltpu.VMEM(tile, jnp.float32),
            pltpu.VMEM((n - 1,) + tile, jnp.float32),
            pltpu.VMEM(tile, jnp.float32),
            pltpu.VMEM((groups - 1,) + tile, jnp.float32),
            pltpu.VMEM(tile, jnp.float32),
            dma((3,)),
            dma(()), dma(()),
            dma((2,)), dma((2,)),
            dma(()), dma((halves,)),
            dma(()), dma((halves, all_rows // BLOCK)),
            dma(()), dma(()),
            dma(()), dma(()),
            dma(()), dma(()),
            dma(()), dma(()),
        ],
        compiler_params=pltpu.CompilerParams(
            collective_id=0, has_side_effects=True, vmem_limit_bytes=32 << 20
        ),
    )(*[hbm(x) for x in (gradient, first_moment, second_moment, basis)], step_number, matrix_ids)
    return place(results)


def solution(mesh):
    in_specs = (
        P("group", "fsdp", None),
        P("group", "fsdp", None),
        P("group", "fsdp", None),
        P("group", "fsdp", None),
        P(),
        P("group"),
    )
    out_specs = (P("group", "fsdp", None), P("group", "fsdp", None), P("group", "fsdp", None))
    return jax.shard_map(local, mesh=mesh, in_specs=in_specs, out_specs=out_specs, check_vma=False)
```

```python
import functools
import math

import jax
import jax.numpy as jnp
from jax import lax
from jax.experimental import pallas as pl
from jax.experimental.pallas import tpu as pltpu
from jax.sharding import PartitionSpec as P

BLOCK = 256


BETA_ONE = 0.95
BETA_TWO = 0.95
ADAM_EPS = 1e-08
HIGHEST = lax.Precision.HIGHEST


def clip_of(local_squares, entries):
    total = lax.psum(local_squares, ("fsdp", "group"))
    return jnp.float32(math.sqrt(entries)) / (jnp.sqrt(total) + 1e-06)


def local_general(gradient, first_moment, second_moment, basis_store, step_number, matrix_ids):
    fsdp_count = lax.axis_size("fsdp")
    group_count = lax.axis_size("group")
    row_count = gradient.shape[1]
    col_count = gradient.shape[2]
    all_rows = row_count * fsdp_count
    col_share = col_count // fsdp_count
    left_blocks = all_rows // BLOCK
    right_blocks = col_count // BLOCK
    entries = all_rows * col_count * group_count
    grad_local = gradient[0].astype(jnp.float32)
    local_squares = jnp.sum(grad_local * grad_local)
    gathered = lax.all_gather(basis_store[0], "fsdp", axis=0, tiled=True)
    owner_rows = basis_store.shape[1]
    owner = (step_number[0] + matrix_ids[0]) % fsdp_count
    ordered_half = jnp.roll(gathered, -owner * owner_rows, axis=0)
    left = ordered_half[:all_rows].astype(jnp.float32).reshape(left_blocks, BLOCK, BLOCK)
    right_half = ordered_half[all_rows:].reshape(right_blocks, BLOCK, BLOCK)
    right = right_half.astype(jnp.float32)
    turned = jnp.einsum(
        "rbj,bjl->rbl",
        gradient[0].reshape(row_count, right_blocks, BLOCK),
        right_half,
        preferred_element_type=jnp.float32,
    )
    turned = clip_of(local_squares, entries) * turned
    outgoing = turned.reshape(row_count, fsdp_count, col_share)
    received = lax.all_to_all(outgoing, "fsdp", split_axis=1, concat_axis=0, tiled=True)
    width = received.shape[2]
    columns = received[:, 0, :].reshape(left_blocks, BLOCK, width)
    rotated = jnp.einsum("bkc,bki->cbi", columns, left, precision=HIGHEST).reshape(width, all_rows)
    count = step_number[0].astype(jnp.float32)
    first_fix = 1.0 - jnp.power(jnp.float32(BETA_ONE), count)
    second_fix = 1.0 - jnp.power(jnp.float32(BETA_TWO), count)
    first_sum = BETA_ONE * first_moment[0].astype(jnp.float32) + (1.0 - BETA_ONE) * rotated
    second_sum = (
        BETA_TWO * second_moment[0].astype(jnp.float32) + (1.0 - BETA_TWO) * rotated * rotated
    )
    direction = first_sum / first_fix / (jnp.sqrt(second_sum / second_fix) + ADAM_EPS)
    backward = jnp.einsum(
        "cbi,bki->cbk", direction.reshape(col_share, left_blocks, BLOCK), left, precision=HIGHEST
    )
    returning = backward.reshape(col_share, fsdp_count, row_count)
    received = lax.all_to_all(returning, "fsdp", split_axis=1, concat_axis=0, tiled=True)
    width = received.shape[2]
    pieces = received[:, 0, :].reshape(right_blocks, BLOCK, width)
    result = jnp.einsum("blr,bjl->rbj", pieces, right, precision=HIGHEST).reshape(width, col_count)
    return (
        result[None].astype(jnp.bfloat16),
        first_sum[None].astype(jnp.bfloat16),
        second_sum[None].astype(jnp.bfloat16),
    )


SLAB = 16
LANES = 128
PARTS = 1
LEAD = 1
MESH = pl.DeviceIdType.MESH


def pieces_of(x):
    high = x.astype(jnp.bfloat16)
    rest = x - high.astype(jnp.float32)
    middle = rest.astype(jnp.bfloat16)
    low = (rest - middle.astype(jnp.float32)).astype(jnp.bfloat16)
    return high, middle, low


def mm(a, b, dims):
    return lax.dot_general(a, b, (dims, ((), ())), preferred_element_type=jnp.float32)


NN = ((1,), (0,))
NT = ((1,), (1,))


def kernel(n, groups, grad, first, second, basis, step, ident, out_u, out_1, out_2,
           held, own, moments, hop, staged, left, right, got, upd, sq_own, sq_f, sq_mid, sq_z, sq_all,
           loc, hop_s, hop_r, left_s, left_r, right_s, right_r, got_s, got_r,
           ret_s, ret_r, f_s, f_r, z_s, z_r, t_s, t_r):
    me = lax.axis_index("fsdp")
    zz = lax.axis_index("group")
    share = grad.shape[1]
    cols = grad.shape[2]
    width = cols // n
    halves = width // BLOCK
    slabs = n // 2
    per_owner = basis.shape[0]
    span = slabs * SLAB
    left_groups = left.shape[0]
    all_rows = share * n
    left_blocks = all_rows // BLOCK
    block_groups = BLOCK // span
    entries = float(share * n * cols * groups)

    core = lax.rem(me, 2)
    per = n // left_blocks
    masks = [m for m in range(2, n, 2)] + [m for m in range(3, n, 2)]
    swapped = [masks[i + 1] if i % 2 == 0 and i + 1 < len(masks) else masks[i - i % 2] for i in range(len(masks))]
    order = list(zip(masks, swapped)) + [(1, 1)]

    def peer(m):
        other = me
        for bit in (1 << i for i in range(n.bit_length() - 1)):
            if m & bit:
                other = other + bit * (1 - 2 * lax.rem(me // bit, 2))
        return other

    def pick(pair):
        a, b = pair
        return a + core * (b - a), peer(a) + core * (peer(b) - peer(a))

    def lanes_of(c):
        return pl.ds(pl.multiple_of(lax.rem(c, 2) * LANES, LANES), LANES)

    def rows_of(c):
        return pl.ds(pl.multiple_of((c // 2) * SLAB, SLAB), SLAB)

    def share_rows(d):
        return pl.ds(pl.multiple_of(d * share, share), share)

    def out_cols(d, t):
        return pl.ds(pl.multiple_of(d * width + t * BLOCK, BLOCK), BLOCK)

    def settle(ref, sem):
        pltpu.make_async_copy(ref, ref, sem).wait()

    def remote(src, dst, ssem, rsem, d):
        return pltpu.make_async_remote_copy(
            src_ref=src, dst_ref=dst, send_sem=ssem, recv_sem=rsem,
            device_id={"fsdp": d}, device_id_type=MESH)

    def across(src, dst, g):
        return pltpu.make_async_remote_copy(
            src_ref=src, dst_ref=dst, send_sem=z_s, recv_sem=z_r,
            device_id={"group": g}, device_id_type=MESH)

    locals_ = [
        pltpu.make_async_copy(grad.at[0], own, loc.at[0]),
        pltpu.make_async_copy(basis, held, loc.at[2]),
        pltpu.make_async_copy(first.at[0], moments.at[0], loc.at[1]),
        pltpu.make_async_copy(second.at[0], moments.at[1], loc.at[1]),
    ]
    for t in range(halves):
        locals_.append(pltpu.make_async_copy(
            grad.at[0, :, out_cols(me, t)], got.at[t, share_rows(me)], got_r.at[t, 0]))
    leads = me == LEAD
    follows = me != LEAD
    roots = jnp.logical_and(leads, zz == 0)
    relays = jnp.logical_and(leads, zz != 0)
    barrier = pltpu.get_barrier_semaphore()
    for k in range(1, n):
        pl.semaphore_signal(barrier, inc=1, device_id={"fsdp": peer(k)}, device_id_type=MESH)

    @pl.when(roots)
    def _():
        for g in range(1, groups):
            pl.semaphore_signal(barrier, inc=1, device_id={"group": g}, device_id_type=MESH)

    for copy in (locals_[1], locals_[0]):
        copy.start()

    @pl.when(relays)
    def _():
        pl.semaphore_wait(barrier, n)

    @pl.when(jnp.logical_not(relays))
    def _():
        pl.semaphore_wait(barrier, n - 1)

    def hop_copy(m, d):
        return remote(held.at[:, d // 2, :, lanes_of(d)], hop.at[me], hop_s, hop_r, d)

    def got_copy(t, m, d):
        return remote(own.at[:, out_cols(d, t)], got.at[t, share_rows(me)],
                      got_s, got_r.at[t, m // per], d)

    def right_copy(t, m, d):
        src = staged.at[pl.ds(left_groups + (d * halves + t) * block_groups, block_groups)]
        dst = right.at[t, :, rows_of(me), lanes_of(me)]
        return remote(src, dst, right_s, right_r.at[t], d)

    def left_copy(m, d):
        return remote(staged.at[pl.ds(0, left_groups)], left.at[:, rows_of(me), lanes_of(me)],
                      left_s.at[0], left_r.at[0], d)

    locals_[1].wait()
    for pair in order:
        hop_copy(*pick(pair)).start()
    pltpu.make_async_copy(held.at[:, me // 2, :, lanes_of(me)], hop.at[me], hop_r).start()
    for copy in locals_[2:]:
        copy.start()
    shared = left.at[:, :, lanes_of(me)]
    sibling = remote(shared, shared, left_s.at[1], left_r.at[1], peer(1))

    def send_got(t, i=None):
        if i is None:
            pairs = order
        else:
            part = [m for m in masks if m // per == i]
            pairs = [(part[j], part[j + 1 - 2 * (j % 2)]) for j in range(len(part))]
            pairs = pairs + ([] if i else [(1, 1)])
        for pair in pairs:
            got_copy(t, *pick(pair)).start()

    locals_[0].wait()
    squares = jnp.zeros((8, LANES), jnp.float32)
    for r in range(0, share, 16):
        rows = own[r:r + 16, :].astype(jnp.float32)
        rows = rows * rows
        rows = rows[0:8] + rows[8:16]
        for c in range(0, cols, LANES):
            squares = squares + rows[:, c:c + LANES]
    sq_own[...] = squares

    @pl.when(follows)
    def _():
        remote(sq_own, sq_f.at[lax.rem(me + n - LEAD - 1, n)], f_s, f_r, LEAD).start()

    send_got(0)

    @pl.when(leads)
    def _():
        settle(sq_f, f_r)
        squares = sq_own[...]
        for k in range(n - 1):
            squares = squares + sq_f[k]
        sq_mid[...] = squares

    @pl.when(relays)
    def _():
        across(sq_mid, sq_z.at[lax.rem(zz + groups - 1, groups)], 0).start()

    settle(hop, hop_r)
    owner = lax.rem(step[0] + ident[0], n)
    left_shards = -(-left_groups // per_owner)

    def stage(q):
        staged[q * per_owner:(q + 1) * per_owner] = hop[lax.rem(owner + q, n)]

    def send_right(t):
        for pair in order:
            right_copy(t, *pick(pair)).start()

    for q in range(left_shards):
        stage(q)
    for m in [m for m in masks if m % 2 == 0]:
        left_copy(m, peer(m)).start()
    for q in range(left_shards, n):
        stage(q)
    send_right(0)
    pltpu.make_async_copy(
        staged.at[pl.ds(0, left_groups)], left.at[:, rows_of(me), lanes_of(me)],
        left_r.at[0]).start()
    for t in range(halves):
        pltpu.make_async_copy(
            staged.at[pl.ds(left_groups + (me * halves + t) * block_groups, block_groups)],
            right.at[t, :, rows_of(me), lanes_of(me)], right_r.at[t]).start()

    @pl.when(roots)
    def _():
        settle(sq_z, z_r)
        squares = sq_mid[...]
        for k in range(groups - 1):
            squares = squares + sq_z[k]
        sq_all[...] = squares
        for g in range(1, groups):
            across(sq_all, sq_all, g).start()

    @pl.when(relays)
    def _():
        settle(sq_all, z_r)

    @pl.when(leads)
    def _():
        for f in range(n):
            if f != LEAD:
                remote(sq_all, sq_all, t_s, t_r, f).start()

    far = list(range(n - 2, 0, -2))
    late = [p for m in far for p in ((m, m + 1), (m + 1, m))] + [(1, 1)]
    for t in range(1, halves):
        for pair in late:
            got_copy(t, *pick(pair)).start()
        send_right(t)

    count = jnp.full((1, 1), step[0].astype(jnp.float32))
    first_inv = 1.0 / (1.0 - jnp.exp(count * jnp.float32(math.log(BETA_ONE))))
    second_inv = 1.0 / (1.0 - jnp.exp(count * jnp.float32(math.log(BETA_TWO))))

    settle(shared, left_r.at[0])
    sibling.start()
    clip = None
    for t in range(halves):
        settle(right.at[t], right_r.at[t])
        rt = right[t].reshape(BLOCK, BLOCK)
        flipped = rt.astype(jnp.float32).T.astype(jnp.bfloat16)
        cut = slice(t * BLOCK, (t + 1) * BLOCK)
        if t == 0:
            sibling.wait_recv()
        for i in reversed(range(left_blocks)):
            b = peer(i * per) // per
            cols_b = pl.ds(pl.multiple_of(b * BLOCK, BLOCK), BLOCK)
            near = range(i * per, (i + 1) * per)
            settle(got.at[t, cols_b], got_r.at[t, i])
            lb = left[pl.ds(b * block_groups, block_groups)].reshape(BLOCK, BLOCK)
            turned = mm(flipped, got[t, cols_b, :], NT)
            rotated = sum(mm(piece, lb, NN) for piece in pieces_of(turned))
            if clip is None:
                @pl.when(follows)
                def _():
                    settle(sq_all, t_r)

                total = jnp.sum(sq_all[...], keepdims=True)
                clip = jnp.float32(math.sqrt(entries)) / (jnp.sqrt(total) + 1e-06)
                settle(moments, loc.at[1])

            rotated = rotated * clip
            first_sum = BETA_ONE * moments[0, cut, cols_b].astype(jnp.float32) + (1.0 - BETA_ONE) * rotated
            second_sum = (BETA_TWO * moments[1, cut, cols_b].astype(jnp.float32)
                          + (1.0 - BETA_TWO) * rotated * rotated)
            out_1[0, cut, cols_b] = first_sum.astype(jnp.bfloat16)
            out_2[0, cut, cols_b] = second_sum.astype(jnp.bfloat16)
            direction = first_sum * first_inv / (jnp.sqrt(second_sum * second_inv) + ADAM_EPS)
            back = sum(mm(rt, piece, NN) for piece in pieces_of(direction))
            result = sum(mm(lb, piece, NT) for piece in pieces_of(back))
            upd[t, cols_b, :] = result.astype(jnp.bfloat16)
            ahead = [m for m in reversed(near) if m > 1 and m % 2 == 0]
            swap = [m + 1 for m in ahead]
            for pair in list(zip(ahead[::-1], swap[::-1])) + list(zip(swap[::-1], ahead[::-1])) + ([] if i else [(1, 1)]):
                d = pick(pair)[1]
                remote(upd.at[t, share_rows(d)], out_u.at[0, :, out_cols(me, t)],
                       ret_s, ret_r, d).start()
            if i == 0:
                pltpu.make_async_copy(upd.at[t, share_rows(me)],
                                      out_u.at[0, :, out_cols(me, t)], ret_r).start()

    settle(hop.at[pl.ds(0, n - 1)], hop_s)

    @pl.when(follows)
    def _():
        settle(sq_own, f_s)

    @pl.when(roots)
    def _():
        settle(sq_z, z_s)

    @pl.when(relays)
    def _():
        settle(sq_mid, z_s)

    @pl.when(leads)
    def _():
        settle(sq_f, t_s)

    settle(staged.at[pl.ds(0, (n // 2 - 1) * left_groups)], left_s.at[0])
    sibling.wait_send()
    settle(staged.at[pl.ds(0, (n - 1) * halves * block_groups)], right_s)
    settle(got.at[:, pl.ds(0, all_rows - share)], got_s)
    settle(upd.at[:, pl.ds(0, all_rows - share)], ret_s)
    settle(out_u, ret_r)


def hbm(x):
    return pltpu.with_memory_space_constraint(x, pltpu.MemorySpace.HBM)


def copy_kernel(a, b, c, x, y, z, sems):
    copies = []
    for src, dst in ((a, x), (b, y), (c, z)):
        rows = src.shape[1] // PARTS
        for i in range(PARTS):
            cut = pl.ds(i * rows, rows)
            copies.append(pltpu.make_async_copy(
                src.at[0, cut], dst.at[0, cut], sems.at[len(copies)]))
    for copy in copies:
        copy.start()
    for copy in copies:
        copy.wait()


def place(arrays):
    return pl.pallas_call(
        copy_kernel,
        out_shape=tuple(jax.ShapeDtypeStruct(a.shape, a.dtype) for a in arrays),
        in_specs=[pl.BlockSpec(memory_space=pltpu.VMEM)] * 3,
        out_specs=(pl.BlockSpec(memory_space=pl.ANY),) * 3,
        scratch_shapes=[pltpu.SemaphoreType.DMA((3 * PARTS,))],
        compiler_params=pltpu.CompilerParams(vmem_limit_bytes=8 << 20),
    )(*arrays)


def fits(gradient, first_moment, basis_store, n):
    if n < 2 or n & (n - 1):
        return False
    span = n // 2 * SLAB
    width = gradient.shape[2] // n
    all_rows = gradient.shape[1] * n
    return (
        BLOCK % span == 0
        and basis_store.shape[1] % span == 0
        and width % BLOCK == 0
        and all_rows % BLOCK == 0
        and n % (all_rows // BLOCK) == 0
        and n // (all_rows // BLOCK) % 2 == 0
        and gradient.shape[1] % SLAB == 0
        and all_rows <= 1024
        and width <= 1024
    )


def local(gradient, first_moment, second_moment, basis_store, step_number, matrix_ids):
    n = lax.axis_size("fsdp")
    groups = lax.axis_size("group")
    if groups < 2 or not fits(gradient, first_moment, basis_store, n):
        return local_general(
            gradient, first_moment, second_moment, basis_store, step_number, matrix_ids
        )
    share, cols = gradient.shape[1:]
    all_rows = share * n
    width = cols // n
    halves = width // BLOCK
    slabs = n // 2
    span = slabs * SLAB
    per_owner = basis_store.shape[1] // span
    basis = basis_store.reshape(per_owner, slabs, SLAB, BLOCK)
    half = jnp.bfloat16
    anywhere = pl.BlockSpec(memory_space=pl.ANY)
    scalar = pl.BlockSpec(memory_space=pltpu.SMEM)
    dma = pltpu.SemaphoreType.DMA
    tile = (8, LANES)
    results = pl.pallas_call(
        functools.partial(kernel, n, groups),
        out_shape=(
            jax.ShapeDtypeStruct(gradient.shape, half),
            jax.ShapeDtypeStruct(first_moment.shape, half),
            jax.ShapeDtypeStruct(second_moment.shape, half),
        ),
        in_specs=[anywhere] * 4 + [scalar] * 2,
        out_specs=(pl.BlockSpec(memory_space=pltpu.VMEM),) * 3,
        scratch_shapes=[
            pltpu.VMEM(basis.shape, half),
            pltpu.VMEM((share, cols), half),
            pltpu.VMEM((2, width, all_rows), half),
            pltpu.VMEM((n, per_owner, SLAB, LANES), half),
            pltpu.VMEM((n * per_owner, SLAB, LANES), half),
            pltpu.VMEM((all_rows // span, span, BLOCK), half),
            pltpu.VMEM((halves, BLOCK // span, span, BLOCK), half),
            pltpu.VMEM((halves, all_rows, BLOCK), half),
            pltpu.VMEM((halves, all_rows, BLOCK), half),
            pltpu.VMEM(tile, jnp.float32),
            pltpu.VMEM((n - 1,) + tile, jnp.float32),
            pltpu.VMEM(tile, jnp.float32),
            pltpu.VMEM((groups - 1,) + tile, jnp.float32),
            pltpu.VMEM(tile, jnp.float32),
            dma((3,)),
            dma(()), dma(()),
            dma((2,)), dma((2,)),
            dma(()), dma((halves,)),
            dma(()), dma((halves, all_rows // BLOCK)),
            dma(()), dma(()),
            dma(()), dma(()),
            dma(()), dma(()),
            dma(()), dma(()),
        ],
        compiler_params=pltpu.CompilerParams(
            collective_id=0, has_side_effects=True, vmem_limit_bytes=32 << 20
        ),
    )(*[hbm(x) for x in (gradient, first_moment, second_moment, basis)], step_number, matrix_ids)
    return place(results)


def solution(mesh):
    in_specs = (
        P("group", "fsdp", None),
        P("group", "fsdp", None),
        P("group", "fsdp", None),
        P("group", "fsdp", None),
        P(),
        P("group"),
    )
    out_specs = (P("group", "fsdp", None), P("group", "fsdp", None), P("group", "fsdp", None))
    return jax.shard_map(local, mesh=mesh, in_specs=in_specs, out_specs=out_specs, check_vma=False)
```

```python
import functools
import math

import jax
import jax.numpy as jnp
from jax import lax
from jax.experimental import pallas as pl
from jax.experimental.pallas import tpu as pltpu
from jax.sharding import PartitionSpec as P

BLOCK = 256


BETA_ONE = 0.95
BETA_TWO = 0.95
ADAM_EPS = 1e-08
HIGHEST = lax.Precision.HIGHEST


def clip_of(local_squares, entries):
    total = lax.psum(local_squares, ("fsdp", "group"))
    return jnp.float32(math.sqrt(entries)) / (jnp.sqrt(total) + 1e-06)


def local_general(gradient, first_moment, second_moment, basis_store, step_number, matrix_ids):
    fsdp_count = lax.axis_size("fsdp")
    group_count = lax.axis_size("group")
    row_count = gradient.shape[1]
    col_count = gradient.shape[2]
    all_rows = row_count * fsdp_count
    col_share = col_count // fsdp_count
    left_blocks = all_rows // BLOCK
    right_blocks = col_count // BLOCK
    entries = all_rows * col_count * group_count
    grad_local = gradient[0].astype(jnp.float32)
    local_squares = jnp.sum(grad_local * grad_local)
    gathered = lax.all_gather(basis_store[0], "fsdp", axis=0, tiled=True)
    owner_rows = basis_store.shape[1]
    owner = (step_number[0] + matrix_ids[0]) % fsdp_count
    ordered_half = jnp.roll(gathered, -owner * owner_rows, axis=0)
    left = ordered_half[:all_rows].astype(jnp.float32).reshape(left_blocks, BLOCK, BLOCK)
    right_half = ordered_half[all_rows:].reshape(right_blocks, BLOCK, BLOCK)
    right = right_half.astype(jnp.float32)
    turned = jnp.einsum(
        "rbj,bjl->rbl",
        gradient[0].reshape(row_count, right_blocks, BLOCK),
        right_half,
        preferred_element_type=jnp.float32,
    )
    turned = clip_of(local_squares, entries) * turned
    outgoing = turned.reshape(row_count, fsdp_count, col_share)
    received = lax.all_to_all(outgoing, "fsdp", split_axis=1, concat_axis=0, tiled=True)
    width = received.shape[2]
    columns = received[:, 0, :].reshape(left_blocks, BLOCK, width)
    rotated = jnp.einsum("bkc,bki->cbi", columns, left, precision=HIGHEST).reshape(width, all_rows)
    count = step_number[0].astype(jnp.float32)
    first_fix = 1.0 - jnp.power(jnp.float32(BETA_ONE), count)
    second_fix = 1.0 - jnp.power(jnp.float32(BETA_TWO), count)
    first_sum = BETA_ONE * first_moment[0].astype(jnp.float32) + (1.0 - BETA_ONE) * rotated
    second_sum = (
        BETA_TWO * second_moment[0].astype(jnp.float32) + (1.0 - BETA_TWO) * rotated * rotated
    )
    direction = first_sum / first_fix / (jnp.sqrt(second_sum / second_fix) + ADAM_EPS)
    backward = jnp.einsum(
        "cbi,bki->cbk", direction.reshape(col_share, left_blocks, BLOCK), left, precision=HIGHEST
    )
    returning = backward.reshape(col_share, fsdp_count, row_count)
    received = lax.all_to_all(returning, "fsdp", split_axis=1, concat_axis=0, tiled=True)
    width = received.shape[2]
    pieces = received[:, 0, :].reshape(right_blocks, BLOCK, width)
    result = jnp.einsum("blr,bjl->rbj", pieces, right, precision=HIGHEST).reshape(width, col_count)
    return (
        result[None].astype(jnp.bfloat16),
        first_sum[None].astype(jnp.bfloat16),
        second_sum[None].astype(jnp.bfloat16),
    )


SLAB = 16
LANES = 128
PARTS = 1
LEAD = 1
MESH = pl.DeviceIdType.MESH


def pieces_of(x):
    high = x.astype(jnp.bfloat16)
    rest = x - high.astype(jnp.float32)
    middle = rest.astype(jnp.bfloat16)
    low = (rest - middle.astype(jnp.float32)).astype(jnp.bfloat16)
    return high, middle, low


def mm(a, b, dims):
    return lax.dot_general(a, b, (dims, ((), ())), preferred_element_type=jnp.float32)


NN = ((1,), (0,))
NT = ((1,), (1,))


def kernel(n, groups, grad, first, second, basis, step, ident, out_u, out_1, out_2,
           held, own, moments, hop, staged, left, right, got, upd, sq_own, sq_f, sq_mid, sq_z, sq_all,
           loc, hop_s, hop_r, left_s, left_r, right_s, right_r, got_s, got_r,
           ret_s, ret_r, f_s, f_r, z_s, z_r):
    me = lax.axis_index("fsdp")
    zz = lax.axis_index("group")
    share = grad.shape[1]
    cols = grad.shape[2]
    width = cols // n
    halves = width // BLOCK
    slabs = n // 2
    per_owner = basis.shape[0]
    span = slabs * SLAB
    left_groups = left.shape[0]
    all_rows = share * n
    left_blocks = all_rows // BLOCK
    block_groups = BLOCK // span
    entries = float(share * n * cols * groups)

    core = lax.rem(me, 2)
    per = n // left_blocks
    masks = [m for m in range(2, n, 2)] + [m for m in range(3, n, 2)]
    swapped = [masks[i + 1] if i % 2 == 0 and i + 1 < len(masks) else masks[i - i % 2] for i in range(len(masks))]
    order = list(zip(masks, swapped)) + [(1, 1)]

    def peer(m):
        other = me
        for bit in (1 << i for i in range(n.bit_length() - 1)):
            if m & bit:
                other = other + bit * (1 - 2 * lax.rem(me // bit, 2))
        return other

    def pick(pair):
        a, b = pair
        return a + core * (b - a), peer(a) + core * (peer(b) - peer(a))

    def lanes_of(c):
        return pl.ds(pl.multiple_of(lax.rem(c, 2) * LANES, LANES), LANES)

    def rows_of(c):
        return pl.ds(pl.multiple_of((c // 2) * SLAB, SLAB), SLAB)

    def share_rows(d):
        return pl.ds(pl.multiple_of(d * share, share), share)

    def out_cols(d, t):
        return pl.ds(pl.multiple_of(d * width + t * BLOCK, BLOCK), BLOCK)

    def settle(ref, sem):
        pltpu.make_async_copy(ref, ref, sem).wait()

    def remote(src, dst, ssem, rsem, d):
        return pltpu.make_async_remote_copy(
            src_ref=src, dst_ref=dst, send_sem=ssem, recv_sem=rsem,
            device_id={"fsdp": d}, device_id_type=MESH)

    def across(src, dst, g):
        return pltpu.make_async_remote_copy(
            src_ref=src, dst_ref=dst, send_sem=z_s, recv_sem=z_r,
            device_id={"group": g}, device_id_type=MESH)

    locals_ = [
        pltpu.make_async_copy(grad.at[0], own, loc.at[0]),
        pltpu.make_async_copy(basis, held, loc.at[2]),
        pltpu.make_async_copy(first.at[0], moments.at[0], loc.at[1]),
        pltpu.make_async_copy(second.at[0], moments.at[1], loc.at[1]),
    ]
    for t in range(halves):
        locals_.append(pltpu.make_async_copy(
            grad.at[0, :, out_cols(me, t)], got.at[t, share_rows(me)], got_r.at[t, 0]))
    leads = me == LEAD
    follows = me != LEAD
    roots = jnp.logical_and(leads, zz == 0)
    relays = jnp.logical_and(leads, zz != 0)
    barrier = pltpu.get_barrier_semaphore()
    locals_[1].start()
    for k in reversed(range(1, n)):
        pl.semaphore_signal(barrier, inc=1, device_id={"fsdp": peer(k)}, device_id_type=MESH)

    @pl.when(roots)
    def _():
        for g in range(1, groups):
            pl.semaphore_signal(barrier, inc=1, device_id={"group": g}, device_id_type=MESH)

    locals_[0].start()

    @pl.when(relays)
    def _():
        pl.semaphore_wait(barrier, n)

    @pl.when(jnp.logical_not(relays))
    def _():
        pl.semaphore_wait(barrier, n - 1)

    def hop_copy(m, d):
        return remote(held.at[:, d // 2, :, lanes_of(d)], hop.at[me], hop_s, hop_r, d)

    def got_copy(t, m, d):
        return remote(own.at[:, out_cols(d, t)], got.at[t, share_rows(me)],
                      got_s, got_r.at[t, m // per], d)

    def right_copy(t, m, d):
        src = staged.at[pl.ds(left_groups + (d * halves + t) * block_groups, block_groups)]
        dst = right.at[t, :, rows_of(me), lanes_of(me)]
        return remote(src, dst, right_s, right_r.at[t], d)

    def left_copy(m, d):
        return remote(staged.at[pl.ds(0, left_groups)], left.at[:, rows_of(me), lanes_of(me)],
                      left_s.at[0], left_r.at[0], d)

    locals_[1].wait()
    for pair in order:
        hop_copy(*pick(pair)).start()
    pltpu.make_async_copy(held.at[:, me // 2, :, lanes_of(me)], hop.at[me], hop_r).start()
    for copy in locals_[2:]:
        copy.start()
    shared = left.at[:, :, lanes_of(me)]
    sibling = remote(shared, shared, left_s.at[1], left_r.at[1], peer(1))

    def send_got(t, i=None):
        if i is None:
            pairs = order
        else:
            part = [m for m in masks if m // per == i]
            pairs = [(part[j], part[j + 1 - 2 * (j % 2)]) for j in range(len(part))]
            pairs = pairs + ([] if i else [(1, 1)])
        for pair in pairs:
            got_copy(t, *pick(pair)).start()

    locals_[0].wait()
    squares = jnp.zeros((8, LANES), jnp.float32)
    for r in range(0, share, 16):
        rows = own[r:r + 16, :].astype(jnp.float32)
        rows = rows * rows
        rows = rows[0:8] + rows[8:16]
        for c in range(0, cols, LANES):
            squares = squares + rows[:, c:c + LANES]
    sq_own[...] = squares

    @pl.when(follows)
    def _():
        remote(sq_own, sq_f.at[lax.rem(me + n - LEAD - 1, n)], f_s, f_r, LEAD).start()

    send_got(0)

    @pl.when(leads)
    def _():
        settle(sq_f, f_r)
        squares = sq_own[...]
        for k in range(n - 1):
            squares = squares + sq_f[k]
        sq_mid[...] = squares

    @pl.when(relays)
    def _():
        across(sq_mid, sq_z.at[lax.rem(zz + groups - 1, groups)], 0).start()

    settle(hop, hop_r)
    owner = lax.rem(step[0] + ident[0], n)
    left_shards = -(-left_groups // per_owner)

    def stage(q):
        staged[q * per_owner:(q + 1) * per_owner] = hop[lax.rem(owner + q, n)]

    def send_right(t):
        for pair in order:
            right_copy(t, *pick(pair)).start()

    for q in range(left_shards):
        stage(q)
    for m in [m for m in masks if m % 2 == 0]:
        left_copy(m, peer(m)).start()
    for q in range(left_shards, n):
        stage(q)
    send_right(0)
    pltpu.make_async_copy(
        staged.at[pl.ds(0, left_groups)], left.at[:, rows_of(me), lanes_of(me)],
        left_r.at[0]).start()
    for t in range(halves):
        pltpu.make_async_copy(
            staged.at[pl.ds(left_groups + (me * halves + t) * block_groups, block_groups)],
            right.at[t, :, rows_of(me), lanes_of(me)], right_r.at[t]).start()

    @pl.when(roots)
    def _():
        settle(sq_z, z_r)
        squares = sq_mid[...]
        for k in range(groups - 1):
            squares = squares + sq_z[k]
        sq_all[...] = squares
        for g in range(1, groups):
            across(sq_all, sq_all, g).start()

    @pl.when(relays)
    def _():
        settle(sq_all, z_r)

    @pl.when(leads)
    def _():
        for f in range(n):
            if f != LEAD:
                remote(sq_all, sq_all, f_s, f_r, f).start()

    far = list(range(n - 2, 0, -2))
    late = [p for m in far for p in ((m, m + 1), (m + 1, m))] + [(1, 1)]
    for t in range(1, halves):
        for pair in late:
            got_copy(t, *pick(pair)).start()
        send_right(t)

    count = jnp.full((1, 1), step[0].astype(jnp.float32))
    first_inv = 1.0 / (1.0 - jnp.exp(count * jnp.float32(math.log(BETA_ONE))))
    second_inv = 1.0 / (1.0 - jnp.exp(count * jnp.float32(math.log(BETA_TWO))))

    settle(shared, left_r.at[0])
    sibling.start()
    clip = None
    for t in range(halves):
        settle(right.at[t], right_r.at[t])
        rt = right[t].reshape(BLOCK, BLOCK)
        flipped = rt.astype(jnp.float32).T.astype(jnp.bfloat16)
        cut = slice(t * BLOCK, (t + 1) * BLOCK)
        if t == 0:
            sibling.wait_recv()
        for i in reversed(range(left_blocks)):
            b = peer(i * per) // per
            cols_b = pl.ds(pl.multiple_of(b * BLOCK, BLOCK), BLOCK)
            near = range(i * per, (i + 1) * per)
            settle(got.at[t, cols_b], got_r.at[t, i])
            lb = left[pl.ds(b * block_groups, block_groups)].reshape(BLOCK, BLOCK)
            turned = mm(flipped, got[t, cols_b, :], NT)
            rotated = sum(mm(piece, lb, NN) for piece in pieces_of(turned))
            if clip is None:
                @pl.when(follows)
                def _():
                    settle(sq_all, f_r)

                total = jnp.sum(sq_all[...], keepdims=True)
                clip = jnp.float32(math.sqrt(entries)) / (jnp.sqrt(total) + 1e-06)
                settle(moments, loc.at[1])

            rotated = rotated * clip
            first_sum = BETA_ONE * moments[0, cut, cols_b].astype(jnp.float32) + (1.0 - BETA_ONE) * rotated
            second_sum = (BETA_TWO * moments[1, cut, cols_b].astype(jnp.float32)
                          + (1.0 - BETA_TWO) * rotated * rotated)
            out_1[0, cut, cols_b] = first_sum.astype(jnp.bfloat16)
            out_2[0, cut, cols_b] = second_sum.astype(jnp.bfloat16)
            direction = first_sum * first_inv / (jnp.sqrt(second_sum * second_inv) + ADAM_EPS)
            back = sum(mm(rt, piece, NN) for piece in pieces_of(direction))
            result = sum(mm(lb, piece, NT) for piece in pieces_of(back))
            upd[t, cols_b, :] = result.astype(jnp.bfloat16)
            ahead = [m for m in reversed(near) if m > 1 and m % 2 == 0]
            swap = [m + 1 for m in ahead]
            for pair in list(zip(ahead[::-1], swap[::-1])) + list(zip(swap[::-1], ahead[::-1])) + ([] if i else [(1, 1)]):
                d = pick(pair)[1]
                remote(upd.at[t, share_rows(d)], out_u.at[0, :, out_cols(me, t)],
                       ret_s, ret_r, d).start()
            if i == 0:
                pltpu.make_async_copy(upd.at[t, share_rows(me)],
                                      out_u.at[0, :, out_cols(me, t)], ret_r).start()

    settle(hop.at[pl.ds(0, n - 1)], hop_s)

    @pl.when(follows)
    def _():
        settle(sq_own, f_s)

    @pl.when(roots)
    def _():
        settle(sq_z, z_s)

    @pl.when(relays)
    def _():
        settle(sq_mid, z_s)

    @pl.when(leads)
    def _():
        settle(sq_f, f_s)

    settle(staged.at[pl.ds(0, (n // 2 - 1) * left_groups)], left_s.at[0])
    sibling.wait_send()
    settle(staged.at[pl.ds(0, (n - 1) * halves * block_groups)], right_s)
    settle(got.at[:, pl.ds(0, all_rows - share)], got_s)
    settle(upd.at[:, pl.ds(0, all_rows - share)], ret_s)
    settle(out_u, ret_r)


def hbm(x):
    return pltpu.with_memory_space_constraint(x, pltpu.MemorySpace.HBM)


def copy_kernel(a, b, c, x, y, z, sems):
    copies = []
    for src, dst in ((a, x), (b, y), (c, z)):
        rows = src.shape[1] // PARTS
        for i in range(PARTS):
            cut = pl.ds(i * rows, rows)
            copies.append(pltpu.make_async_copy(
                src.at[0, cut], dst.at[0, cut], sems.at[len(copies)]))
    for copy in copies:
        copy.start()
    for copy in copies:
        copy.wait()


def place(arrays):
    return pl.pallas_call(
        copy_kernel,
        out_shape=tuple(jax.ShapeDtypeStruct(a.shape, a.dtype) for a in arrays),
        in_specs=[pl.BlockSpec(memory_space=pltpu.VMEM)] * 3,
        out_specs=(pl.BlockSpec(memory_space=pl.ANY),) * 3,
        scratch_shapes=[pltpu.SemaphoreType.DMA((3 * PARTS,))],
        compiler_params=pltpu.CompilerParams(vmem_limit_bytes=8 << 20),
    )(*arrays)


def fits(gradient, first_moment, basis_store, n):
    if n < 2 or n & (n - 1):
        return False
    span = n // 2 * SLAB
    width = gradient.shape[2] // n
    all_rows = gradient.shape[1] * n
    return (
        BLOCK % span == 0
        and basis_store.shape[1] % span == 0
        and width % BLOCK == 0
        and all_rows % BLOCK == 0
        and n % (all_rows // BLOCK) == 0
        and n // (all_rows // BLOCK) % 2 == 0
        and gradient.shape[1] % SLAB == 0
        and all_rows <= 1024
        and width <= 1024
    )


def local(gradient, first_moment, second_moment, basis_store, step_number, matrix_ids):
    n = lax.axis_size("fsdp")
    groups = lax.axis_size("group")
    if groups < 2 or not fits(gradient, first_moment, basis_store, n):
        return local_general(
            gradient, first_moment, second_moment, basis_store, step_number, matrix_ids
        )
    share, cols = gradient.shape[1:]
    all_rows = share * n
    width = cols // n
    halves = width // BLOCK
    slabs = n // 2
    span = slabs * SLAB
    per_owner = basis_store.shape[1] // span
    basis = basis_store.reshape(per_owner, slabs, SLAB, BLOCK)
    half = jnp.bfloat16
    anywhere = pl.BlockSpec(memory_space=pl.ANY)
    scalar = pl.BlockSpec(memory_space=pltpu.SMEM)
    dma = pltpu.SemaphoreType.DMA
    tile = (8, LANES)
    results = pl.pallas_call(
        functools.partial(kernel, n, groups),
        out_shape=(
            jax.ShapeDtypeStruct(gradient.shape, half),
            jax.ShapeDtypeStruct(first_moment.shape, half),
            jax.ShapeDtypeStruct(second_moment.shape, half),
        ),
        in_specs=[anywhere] * 4 + [scalar] * 2,
        out_specs=(pl.BlockSpec(memory_space=pltpu.VMEM),) * 3,
        scratch_shapes=[
            pltpu.VMEM(basis.shape, half),
            pltpu.VMEM((share, cols), half),
            pltpu.VMEM((2, width, all_rows), half),
            pltpu.VMEM((n, per_owner, SLAB, LANES), half),
            pltpu.VMEM((n * per_owner, SLAB, LANES), half),
            pltpu.VMEM((all_rows // span, span, BLOCK), half),
            pltpu.VMEM((halves, BLOCK // span, span, BLOCK), half),
            pltpu.VMEM((halves, all_rows, BLOCK), half),
            pltpu.VMEM((halves, all_rows, BLOCK), half),
            pltpu.VMEM(tile, jnp.float32),
            pltpu.VMEM((n - 1,) + tile, jnp.float32),
            pltpu.VMEM(tile, jnp.float32),
            pltpu.VMEM((groups - 1,) + tile, jnp.float32),
            pltpu.VMEM(tile, jnp.float32),
            dma((3,)),
            dma(()), dma(()),
            dma((2,)), dma((2,)),
            dma(()), dma((halves,)),
            dma(()), dma((halves, all_rows // BLOCK)),
            dma(()), dma(()),
            dma(()), dma(()),
            dma(()), dma(()),
        ],
        compiler_params=pltpu.CompilerParams(
            collective_id=0, has_side_effects=True, vmem_limit_bytes=32 << 20
        ),
    )(*[hbm(x) for x in (gradient, first_moment, second_moment, basis)], step_number, matrix_ids)
    return place(results)


def solution(mesh):
    in_specs = (
        P("group", "fsdp", None),
        P("group", "fsdp", None),
        P("group", "fsdp", None),
        P("group", "fsdp", None),
        P(),
        P("group"),
    )
    out_specs = (P("group", "fsdp", None), P("group", "fsdp", None), P("group", "fsdp", None))
    return jax.shard_map(local, mesh=mesh, in_specs=in_specs, out_specs=out_specs, check_vma=False)
```

```python
import functools
import math

import jax
import jax.numpy as jnp
from jax import lax
from jax.experimental import pallas as pl
from jax.experimental.pallas import tpu as pltpu
from jax.sharding import PartitionSpec as P

BLOCK = 256


BETA_ONE = 0.95
BETA_TWO = 0.95
ADAM_EPS = 1e-08
HIGHEST = lax.Precision.HIGHEST


def clip_of(local_squares, entries):
    total = lax.psum(local_squares, ("fsdp", "group"))
    return jnp.float32(math.sqrt(entries)) / (jnp.sqrt(total) + 1e-06)


def local_general(gradient, first_moment, second_moment, basis_store, step_number, matrix_ids):
    fsdp_count = lax.axis_size("fsdp")
    group_count = lax.axis_size("group")
    row_count = gradient.shape[1]
    col_count = gradient.shape[2]
    all_rows = row_count * fsdp_count
    col_share = col_count // fsdp_count
    left_blocks = all_rows // BLOCK
    right_blocks = col_count // BLOCK
    entries = all_rows * col_count * group_count
    grad_local = gradient[0].astype(jnp.float32)
    local_squares = jnp.sum(grad_local * grad_local)
    gathered = lax.all_gather(basis_store[0], "fsdp", axis=0, tiled=True)
    owner_rows = basis_store.shape[1]
    owner = (step_number[0] + matrix_ids[0]) % fsdp_count
    ordered_half = jnp.roll(gathered, -owner * owner_rows, axis=0)
    left = ordered_half[:all_rows].astype(jnp.float32).reshape(left_blocks, BLOCK, BLOCK)
    right_half = ordered_half[all_rows:].reshape(right_blocks, BLOCK, BLOCK)
    right = right_half.astype(jnp.float32)
    turned = jnp.einsum(
        "rbj,bjl->rbl",
        gradient[0].reshape(row_count, right_blocks, BLOCK),
        right_half,
        preferred_element_type=jnp.float32,
    )
    turned = clip_of(local_squares, entries) * turned
    outgoing = turned.reshape(row_count, fsdp_count, col_share)
    received = lax.all_to_all(outgoing, "fsdp", split_axis=1, concat_axis=0, tiled=True)
    width = received.shape[2]
    columns = received[:, 0, :].reshape(left_blocks, BLOCK, width)
    rotated = jnp.einsum("bkc,bki->cbi", columns, left, precision=HIGHEST).reshape(width, all_rows)
    count = step_number[0].astype(jnp.float32)
    first_fix = 1.0 - jnp.power(jnp.float32(BETA_ONE), count)
    second_fix = 1.0 - jnp.power(jnp.float32(BETA_TWO), count)
    first_sum = BETA_ONE * first_moment[0].astype(jnp.float32) + (1.0 - BETA_ONE) * rotated
    second_sum = (
        BETA_TWO * second_moment[0].astype(jnp.float32) + (1.0 - BETA_TWO) * rotated * rotated
    )
    direction = first_sum / first_fix / (jnp.sqrt(second_sum / second_fix) + ADAM_EPS)
    backward = jnp.einsum(
        "cbi,bki->cbk", direction.reshape(col_share, left_blocks, BLOCK), left, precision=HIGHEST
    )
    returning = backward.reshape(col_share, fsdp_count, row_count)
    received = lax.all_to_all(returning, "fsdp", split_axis=1, concat_axis=0, tiled=True)
    width = received.shape[2]
    pieces = received[:, 0, :].reshape(right_blocks, BLOCK, width)
    result = jnp.einsum("blr,bjl->rbj", pieces, right, precision=HIGHEST).reshape(width, col_count)
    return (
        result[None].astype(jnp.bfloat16),
        first_sum[None].astype(jnp.bfloat16),
        second_sum[None].astype(jnp.bfloat16),
    )


SLAB = 16
LANES = 128
PARTS = 1
LEAD = 1
MESH = pl.DeviceIdType.MESH


def pieces_of(x):
    high = x.astype(jnp.bfloat16)
    rest = x - high.astype(jnp.float32)
    middle = rest.astype(jnp.bfloat16)
    low = (rest - middle.astype(jnp.float32)).astype(jnp.bfloat16)
    return high, middle, low


def mm(a, b, dims):
    return lax.dot_general(a, b, (dims, ((), ())), preferred_element_type=jnp.float32)


NN = ((1,), (0,))
NT = ((1,), (1,))


def kernel(n, groups, grad, first, second, basis, step, ident, out_u, out_1, out_2,
           held, own, moments, hop, staged, left, right, got, upd, sq_own, sq_f, sq_mid, sq_z, sq_all,
           loc, hop_s, hop_r, left_s, left_r, right_s, right_r, got_s, got_r,
           ret_s, ret_r, f_s, f_r, z_s, z_r):
    me = lax.axis_index("fsdp")
    zz = lax.axis_index("group")
    share = grad.shape[1]
    cols = grad.shape[2]
    width = cols // n
    halves = width // BLOCK
    slabs = n // 2
    per_owner = basis.shape[0]
    span = slabs * SLAB
    left_groups = left.shape[1]
    all_rows = share * n
    left_blocks = all_rows // BLOCK
    block_groups = BLOCK // span
    entries = float(share * n * cols * groups)

    core = lax.rem(me, 2)
    per = n // left_blocks
    masks = [m for m in range(2, n, 2)] + [m for m in range(3, n, 2)]
    swapped = [masks[i + 1] if i % 2 == 0 and i + 1 < len(masks) else masks[i - i % 2] for i in range(len(masks))]
    order = list(zip(masks, swapped)) + [(1, 1)]

    def peer(m):
        other = me
        for bit in (1 << i for i in range(n.bit_length() - 1)):
            if m & bit:
                other = other + bit * (1 - 2 * lax.rem(me // bit, 2))
        return other

    def pick(pair):
        a, b = pair
        return a + core * (b - a), peer(a) + core * (peer(b) - peer(a))

    def lanes_of(c):
        return pl.ds(pl.multiple_of(lax.rem(c, 2) * LANES, LANES), LANES)

    def rows_of(c):
        return pl.ds(pl.multiple_of((c // 2) * SLAB, SLAB), SLAB)

    def share_rows(d):
        return pl.ds(pl.multiple_of(d * share, share), share)

    def out_cols(d, t):
        return pl.ds(pl.multiple_of(d * width + t * BLOCK, BLOCK), BLOCK)

    def joined(parts):
        return jnp.concatenate([part.reshape(BLOCK, LANES) for part in parts], axis=1)

    def settle(ref, sem):
        pltpu.make_async_copy(ref, ref, sem).wait()

    def remote(src, dst, ssem, rsem, d):
        return pltpu.make_async_remote_copy(
            src_ref=src, dst_ref=dst, send_sem=ssem, recv_sem=rsem,
            device_id={"fsdp": d}, device_id_type=MESH)

    def across(src, dst, g):
        return pltpu.make_async_remote_copy(
            src_ref=src, dst_ref=dst, send_sem=z_s, recv_sem=z_r,
            device_id={"group": g}, device_id_type=MESH)

    locals_ = [
        pltpu.make_async_copy(grad.at[0], own, loc.at[0]),
        pltpu.make_async_copy(basis, held, loc.at[2]),
        pltpu.make_async_copy(first.at[0], moments.at[0], loc.at[1]),
        pltpu.make_async_copy(second.at[0], moments.at[1], loc.at[1]),
    ]
    for t in range(halves):
        locals_.append(pltpu.make_async_copy(
            grad.at[0, :, out_cols(me, t)], got.at[t, share_rows(me)], got_r.at[t, 0]))
    leads = me == LEAD
    follows = me != LEAD
    roots = jnp.logical_and(leads, zz == 0)
    relays = jnp.logical_and(leads, zz != 0)
    barrier = pltpu.get_barrier_semaphore()
    locals_[1].start()
    for k in reversed(range(1, n)):
        pl.semaphore_signal(barrier, inc=1, device_id={"fsdp": peer(k)}, device_id_type=MESH)

    @pl.when(roots)
    def _():
        for g in range(1, groups):
            pl.semaphore_signal(barrier, inc=1, device_id={"group": g}, device_id_type=MESH)

    locals_[0].start()

    @pl.when(relays)
    def _():
        pl.semaphore_wait(barrier, n)

    @pl.when(jnp.logical_not(relays))
    def _():
        pl.semaphore_wait(barrier, n - 1)

    def hop_copy(m, d):
        return remote(held.at[:, d // 2, :, lanes_of(d)], hop.at[me], hop_s, hop_r, d)

    def got_copy(t, m, d):
        return remote(own.at[:, out_cols(d, t)], got.at[t, share_rows(me)],
                      got_s, got_r.at[t, m // per], d)

    def right_copy(t, m, d):
        src = staged.at[pl.ds(left_groups + (d * halves + t) * block_groups, block_groups)]
        dst = right.at[t, lax.rem(me, 2), :, rows_of(me)]
        return remote(src, dst, right_s, right_r.at[t], d)

    def left_copy(m, d):
        return remote(staged.at[pl.ds(0, left_groups)], left.at[lax.rem(me, 2), :, rows_of(me)],
                      left_s.at[0], left_r.at[0], d)

    locals_[1].wait()
    for pair in order:
        hop_copy(*pick(pair)).start()
    pltpu.make_async_copy(held.at[:, me // 2, :, lanes_of(me)], hop.at[me], hop_r).start()
    for copy in locals_[2:]:
        copy.start()
    shared = left.at[lax.rem(me, 2)]
    sibling = remote(shared, shared, left_s.at[1], left_r.at[1], peer(1))

    def send_got(t, i=None):
        if i is None:
            pairs = order
        else:
            part = [m for m in masks if m // per == i]
            pairs = [(part[j], part[j + 1 - 2 * (j % 2)]) for j in range(len(part))]
            pairs = pairs + ([] if i else [(1, 1)])
        for pair in pairs:
            got_copy(t, *pick(pair)).start()

    locals_[0].wait()
    squares = jnp.zeros((8, LANES), jnp.float32)
    for r in range(0, share, 16):
        rows = own[r:r + 16, :].astype(jnp.float32)
        rows = rows * rows
        rows = rows[0:8] + rows[8:16]
        for c in range(0, cols, LANES):
            squares = squares + rows[:, c:c + LANES]
    sq_own[...] = squares

    @pl.when(follows)
    def _():
        remote(sq_own, sq_f.at[lax.rem(me + n - LEAD - 1, n)], f_s, f_r, LEAD).start()

    send_got(0)

    @pl.when(leads)
    def _():
        settle(sq_f, f_r)
        squares = sq_own[...]
        for k in range(n - 1):
            squares = squares + sq_f[k]
        sq_mid[...] = squares

    @pl.when(relays)
    def _():
        across(sq_mid, sq_z.at[lax.rem(zz + groups - 1, groups)], 0).start()

    settle(hop, hop_r)
    owner = lax.rem(step[0] + ident[0], n)
    left_shards = -(-left_groups // per_owner)

    def stage(q):
        staged[q * per_owner:(q + 1) * per_owner] = hop[lax.rem(owner + q, n)]

    def send_right(t):
        for pair in order:
            right_copy(t, *pick(pair)).start()

    for q in range(left_shards):
        stage(q)
    for m in [m for m in masks if m % 2 == 0]:
        left_copy(m, peer(m)).start()
    for q in range(left_shards, n):
        stage(q)
    send_right(0)
    pltpu.make_async_copy(
        staged.at[pl.ds(0, left_groups)], left.at[lax.rem(me, 2), :, rows_of(me)],
        left_r.at[0]).start()
    for t in range(halves):
        pltpu.make_async_copy(
            staged.at[pl.ds(left_groups + (me * halves + t) * block_groups, block_groups)],
            right.at[t, lax.rem(me, 2), :, rows_of(me)], right_r.at[t]).start()

    @pl.when(roots)
    def _():
        settle(sq_z, z_r)
        squares = sq_mid[...]
        for k in range(groups - 1):
            squares = squares + sq_z[k]
        sq_all[...] = squares
        for g in range(1, groups):
            across(sq_all, sq_all, g).start()

    @pl.when(relays)
    def _():
        settle(sq_all, z_r)

    @pl.when(leads)
    def _():
        for f in range(n):
            if f != LEAD:
                remote(sq_all, sq_all, f_s, f_r, f).start()

    far = list(range(n - 2, 0, -2))
    late = [p for m in far for p in ((m, m + 1), (m + 1, m))] + [(1, 1)]
    for t in range(1, halves):
        for pair in late:
            got_copy(t, *pick(pair)).start()
        send_right(t)

    count = jnp.full((1, 1), step[0].astype(jnp.float32))
    first_inv = 1.0 / (1.0 - jnp.exp(count * jnp.float32(math.log(BETA_ONE))))
    second_inv = 1.0 / (1.0 - jnp.exp(count * jnp.float32(math.log(BETA_TWO))))

    settle(shared, left_r.at[0])
    sibling.start()
    clip = None
    for t in range(halves):
        settle(right.at[t], right_r.at[t])
        rt = joined([right[t, half] for half in range(2)])
        flipped = rt.astype(jnp.float32).T.astype(jnp.bfloat16)
        cut = slice(t * BLOCK, (t + 1) * BLOCK)
        if t == 0:
            sibling.wait_recv()
        for i in reversed(range(left_blocks)):
            b = peer(i * per) // per
            cols_b = pl.ds(pl.multiple_of(b * BLOCK, BLOCK), BLOCK)
            near = range(i * per, (i + 1) * per)
            settle(got.at[t, cols_b], got_r.at[t, i])
            lb = joined([left[half, pl.ds(b * block_groups, block_groups)] for half in range(2)])
            turned = mm(flipped, got[t, cols_b, :], NT)
            rotated = sum(mm(piece, lb, NN) for piece in pieces_of(turned))
            if clip is None:
                @pl.when(follows)
                def _():
                    settle(sq_all, f_r)

                total = jnp.sum(sq_all[...], keepdims=True)
                clip = jnp.float32(math.sqrt(entries)) / (jnp.sqrt(total) + 1e-06)
                settle(moments, loc.at[1])

            rotated = rotated * clip
            first_sum = BETA_ONE * moments[0, cut, cols_b].astype(jnp.float32) + (1.0 - BETA_ONE) * rotated
            second_sum = (BETA_TWO * moments[1, cut, cols_b].astype(jnp.float32)
                          + (1.0 - BETA_TWO) * rotated * rotated)
            out_1[0, cut, cols_b] = first_sum.astype(jnp.bfloat16)
            out_2[0, cut, cols_b] = second_sum.astype(jnp.bfloat16)
            direction = first_sum * first_inv / (jnp.sqrt(second_sum * second_inv) + ADAM_EPS)
            back = sum(mm(rt, piece, NN) for piece in pieces_of(direction))
            result = sum(mm(lb, piece, NT) for piece in pieces_of(back))
            upd[t, cols_b, :] = result.astype(jnp.bfloat16)
            ahead = [m for m in reversed(near) if m > 1 and m % 2 == 0]
            swap = [m + 1 for m in ahead]
            for pair in list(zip(ahead, swap)) + list(zip(swap, ahead)) + ([] if i else [(1, 1)]):
                d = pick(pair)[1]
                remote(upd.at[t, share_rows(d)], out_u.at[0, :, out_cols(me, t)],
                       ret_s, ret_r, d).start()
            if i == 0:
                pltpu.make_async_copy(upd.at[t, share_rows(me)],
                                      out_u.at[0, :, out_cols(me, t)], ret_r).start()

    settle(hop.at[pl.ds(0, n - 1)], hop_s)

    @pl.when(follows)
    def _():
        settle(sq_own, f_s)

    @pl.when(roots)
    def _():
        settle(sq_z, z_s)

    @pl.when(relays)
    def _():
        settle(sq_mid, z_s)

    @pl.when(leads)
    def _():
        settle(sq_f, f_s)

    settle(staged.at[pl.ds(0, (n // 2 - 1) * left_groups)], left_s.at[0])
    sibling.wait_send()
    settle(staged.at[pl.ds(0, (n - 1) * halves * block_groups)], right_s)
    settle(got.at[:, pl.ds(0, all_rows - share)], got_s)
    settle(upd.at[:, pl.ds(0, all_rows - share)], ret_s)
    settle(out_u, ret_r)


def hbm(x):
    return pltpu.with_memory_space_constraint(x, pltpu.MemorySpace.HBM)


def copy_kernel(a, b, c, x, y, z, sems):
    copies = []
    for src, dst in ((a, x), (b, y), (c, z)):
        rows = src.shape[1] // PARTS
        for i in range(PARTS):
            cut = pl.ds(i * rows, rows)
            copies.append(pltpu.make_async_copy(
                src.at[0, cut], dst.at[0, cut], sems.at[len(copies)]))
    for copy in copies:
        copy.start()
    for copy in copies:
        copy.wait()


def place(arrays):
    return pl.pallas_call(
        copy_kernel,
        out_shape=tuple(jax.ShapeDtypeStruct(a.shape, a.dtype) for a in arrays),
        in_specs=[pl.BlockSpec(memory_space=pltpu.VMEM)] * 3,
        out_specs=(pl.BlockSpec(memory_space=pl.ANY),) * 3,
        scratch_shapes=[pltpu.SemaphoreType.DMA((3 * PARTS,))],
        compiler_params=pltpu.CompilerParams(vmem_limit_bytes=8 << 20),
    )(*arrays)


def fits(gradient, first_moment, basis_store, n):
    if n < 2 or n & (n - 1):
        return False
    span = n // 2 * SLAB
    width = gradient.shape[2] // n
    all_rows = gradient.shape[1] * n
    return (
        BLOCK % span == 0
        and basis_store.shape[1] % span == 0
        and width % BLOCK == 0
        and all_rows % BLOCK == 0
        and n % (all_rows // BLOCK) == 0
        and n // (all_rows // BLOCK) % 2 == 0
        and gradient.shape[1] % SLAB == 0
        and all_rows <= 1024
        and width <= 1024
    )


def local(gradient, first_moment, second_moment, basis_store, step_number, matrix_ids):
    n = lax.axis_size("fsdp")
    groups = lax.axis_size("group")
    if groups < 2 or not fits(gradient, first_moment, basis_store, n):
        return local_general(
            gradient, first_moment, second_moment, basis_store, step_number, matrix_ids
        )
    share, cols = gradient.shape[1:]
    all_rows = share * n
    width = cols // n
    halves = width // BLOCK
    slabs = n // 2
    span = slabs * SLAB
    per_owner = basis_store.shape[1] // span
    basis = basis_store.reshape(per_owner, slabs, SLAB, BLOCK)
    half = jnp.bfloat16
    anywhere = pl.BlockSpec(memory_space=pl.ANY)
    scalar = pl.BlockSpec(memory_space=pltpu.SMEM)
    dma = pltpu.SemaphoreType.DMA
    tile = (8, LANES)
    results = pl.pallas_call(
        functools.partial(kernel, n, groups),
        out_shape=(
            jax.ShapeDtypeStruct(gradient.shape, half),
            jax.ShapeDtypeStruct(first_moment.shape, half),
            jax.ShapeDtypeStruct(second_moment.shape, half),
        ),
        in_specs=[anywhere] * 4 + [scalar] * 2,
        out_specs=(pl.BlockSpec(memory_space=pltpu.VMEM),) * 3,
        scratch_shapes=[
            pltpu.VMEM(basis.shape, half),
            pltpu.VMEM((share, cols), half),
            pltpu.VMEM((2, width, all_rows), half),
            pltpu.VMEM((n, per_owner, SLAB, LANES), half),
            pltpu.VMEM((n * per_owner, SLAB, LANES), half),
            pltpu.VMEM((2, all_rows // span, span, LANES), half),
            pltpu.VMEM((halves, 2, BLOCK // span, span, LANES), half),
            pltpu.VMEM((halves, all_rows, BLOCK), half),
            pltpu.VMEM((halves, all_rows, BLOCK), half),
            pltpu.VMEM(tile, jnp.float32),
            pltpu.VMEM((n - 1,) + tile, jnp.float32),
            pltpu.VMEM(tile, jnp.float32),
            pltpu.VMEM((groups - 1,) + tile, jnp.float32),
            pltpu.VMEM(tile, jnp.float32),
            dma((3,)),
            dma(()), dma(()),
            dma((2,)), dma((2,)),
            dma(()), dma((halves,)),
            dma(()), dma((halves, all_rows // BLOCK)),
            dma(()), dma(()),
            dma(()), dma(()),
            dma(()), dma(()),
        ],
        compiler_params=pltpu.CompilerParams(
            collective_id=0, has_side_effects=True, vmem_limit_bytes=32 << 20
        ),
    )(*[hbm(x) for x in (gradient, first_moment, second_moment, basis)], step_number, matrix_ids)
    return place(results)


def solution(mesh):
    in_specs = (
        P("group", "fsdp", None),
        P("group", "fsdp", None),
        P("group", "fsdp", None),
        P("group", "fsdp", None),
        P(),
        P("group"),
    )
    out_specs = (P("group", "fsdp", None), P("group", "fsdp", None), P("group", "fsdp", None))
    return jax.shard_map(local, mesh=mesh, in_specs=in_specs, out_specs=out_specs, check_vma=False)
```

```python
import functools
import math

import jax
import jax.numpy as jnp
from jax import lax
from jax.experimental import pallas as pl
from jax.experimental.pallas import tpu as pltpu
from jax.sharding import PartitionSpec as P

BLOCK = 256


BETA_ONE = 0.95
BETA_TWO = 0.95
ADAM_EPS = 1e-08
HIGHEST = lax.Precision.HIGHEST


def clip_of(local_squares, entries):
    total = lax.psum(local_squares, ("fsdp", "group"))
    return jnp.float32(math.sqrt(entries)) / (jnp.sqrt(total) + 1e-06)


def local_general(gradient, first_moment, second_moment, basis_store, step_number, matrix_ids):
    fsdp_count = lax.axis_size("fsdp")
    group_count = lax.axis_size("group")
    row_count = gradient.shape[1]
    col_count = gradient.shape[2]
    all_rows = row_count * fsdp_count
    col_share = col_count // fsdp_count
    left_blocks = all_rows // BLOCK
    right_blocks = col_count // BLOCK
    entries = all_rows * col_count * group_count
    grad_local = gradient[0].astype(jnp.float32)
    local_squares = jnp.sum(grad_local * grad_local)
    gathered = lax.all_gather(basis_store[0], "fsdp", axis=0, tiled=True)
    owner_rows = basis_store.shape[1]
    owner = (step_number[0] + matrix_ids[0]) % fsdp_count
    ordered_half = jnp.roll(gathered, -owner * owner_rows, axis=0)
    left = ordered_half[:all_rows].astype(jnp.float32).reshape(left_blocks, BLOCK, BLOCK)
    right_half = ordered_half[all_rows:].reshape(right_blocks, BLOCK, BLOCK)
    right = right_half.astype(jnp.float32)
    turned = jnp.einsum(
        "rbj,bjl->rbl",
        gradient[0].reshape(row_count, right_blocks, BLOCK),
        right_half,
        preferred_element_type=jnp.float32,
    )
    turned = clip_of(local_squares, entries) * turned
    outgoing = turned.reshape(row_count, fsdp_count, col_share)
    received = lax.all_to_all(outgoing, "fsdp", split_axis=1, concat_axis=0, tiled=True)
    width = received.shape[2]
    columns = received[:, 0, :].reshape(left_blocks, BLOCK, width)
    rotated = jnp.einsum("bkc,bki->cbi", columns, left, precision=HIGHEST).reshape(width, all_rows)
    count = step_number[0].astype(jnp.float32)
    first_fix = 1.0 - jnp.power(jnp.float32(BETA_ONE), count)
    second_fix = 1.0 - jnp.power(jnp.float32(BETA_TWO), count)
    first_sum = BETA_ONE * first_moment[0].astype(jnp.float32) + (1.0 - BETA_ONE) * rotated
    second_sum = (
        BETA_TWO * second_moment[0].astype(jnp.float32) + (1.0 - BETA_TWO) * rotated * rotated
    )
    direction = first_sum / first_fix / (jnp.sqrt(second_sum / second_fix) + ADAM_EPS)
    backward = jnp.einsum(
        "cbi,bki->cbk", direction.reshape(col_share, left_blocks, BLOCK), left, precision=HIGHEST
    )
    returning = backward.reshape(col_share, fsdp_count, row_count)
    received = lax.all_to_all(returning, "fsdp", split_axis=1, concat_axis=0, tiled=True)
    width = received.shape[2]
    pieces = received[:, 0, :].reshape(right_blocks, BLOCK, width)
    result = jnp.einsum("blr,bjl->rbj", pieces, right, precision=HIGHEST).reshape(width, col_count)
    return (
        result[None].astype(jnp.bfloat16),
        first_sum[None].astype(jnp.bfloat16),
        second_sum[None].astype(jnp.bfloat16),
    )


SLAB = 16
LANES = 128
PARTS = 1
LEAD = 1
MESH = pl.DeviceIdType.MESH


def pieces_of(x):
    high = x.astype(jnp.bfloat16)
    rest = x - high.astype(jnp.float32)
    middle = rest.astype(jnp.bfloat16)
    low = (rest - middle.astype(jnp.float32)).astype(jnp.bfloat16)
    return high, middle, low


def mm(a, b, dims):
    return lax.dot_general(a, b, (dims, ((), ())), preferred_element_type=jnp.float32)


NN = ((1,), (0,))
NT = ((1,), (1,))


def kernel(n, groups, grad, first, second, basis, step, ident, out_u, out_1, out_2,
           held, own, moments, hop, staged, left, right, got, upd, sq_own, sq_f, sq_mid, sq_z, sq_all,
           loc, hop_s, hop_r, left_s, left_r, right_s, right_r, got_s, got_r,
           ret_s, ret_r, f_s, f_r, z_s, z_r):
    me = lax.axis_index("fsdp")
    zz = lax.axis_index("group")
    share = grad.shape[1]
    cols = grad.shape[2]
    width = cols // n
    halves = width // BLOCK
    slabs = n // 2
    per_owner = basis.shape[0]
    span = slabs * SLAB
    left_groups = left.shape[0]
    all_rows = share * n
    left_blocks = all_rows // BLOCK
    block_groups = BLOCK // span
    entries = float(share * n * cols * groups)

    core = lax.rem(me, 2)
    per = n // left_blocks
    masks = [m for m in range(2, n, 2)] + [m for m in range(3, n, 2)]
    swapped = [masks[i + 1] if i % 2 == 0 and i + 1 < len(masks) else masks[i - i % 2] for i in range(len(masks))]
    order = list(zip(masks, swapped)) + [(1, 1)]

    def peer(m):
        other = me
        for bit in (1 << i for i in range(n.bit_length() - 1)):
            if m & bit:
                other = other + bit * (1 - 2 * lax.rem(me // bit, 2))
        return other

    def pick(pair):
        a, b = pair
        return a + core * (b - a), peer(a) + core * (peer(b) - peer(a))

    def lanes_of(c):
        return pl.ds(pl.multiple_of(lax.rem(c, 2) * LANES, LANES), LANES)

    def rows_of(c):
        return pl.ds(pl.multiple_of((c // 2) * SLAB, SLAB), SLAB)

    def share_rows(d):
        return pl.ds(pl.multiple_of(d * share, share), share)

    def out_cols(d, t):
        return pl.ds(pl.multiple_of(d * width + t * BLOCK, BLOCK), BLOCK)

    def settle(ref, sem):
        pltpu.make_async_copy(ref, ref, sem).wait()

    def remote(src, dst, ssem, rsem, d):
        return pltpu.make_async_remote_copy(
            src_ref=src, dst_ref=dst, send_sem=ssem, recv_sem=rsem,
            device_id={"fsdp": d}, device_id_type=MESH)

    def across(src, dst, g):
        return pltpu.make_async_remote_copy(
            src_ref=src, dst_ref=dst, send_sem=z_s, recv_sem=z_r,
            device_id={"group": g}, device_id_type=MESH)

    locals_ = [
        pltpu.make_async_copy(grad.at[0], own, loc.at[0]),
        pltpu.make_async_copy(basis, held, loc.at[2]),
        pltpu.make_async_copy(first.at[0], moments.at[0], loc.at[1]),
        pltpu.make_async_copy(second.at[0], moments.at[1], loc.at[1]),
    ]
    for t in range(halves):
        locals_.append(pltpu.make_async_copy(
            grad.at[0, :, out_cols(me, t)], got.at[t, share_rows(me)], got_r.at[t, 0]))
    leads = me == LEAD
    follows = me != LEAD
    roots = jnp.logical_and(leads, zz == 0)
    relays = jnp.logical_and(leads, zz != 0)
    barrier = pltpu.get_barrier_semaphore()
    locals_[1].start()
    for k in reversed(range(1, n)):
        pl.semaphore_signal(barrier, inc=1, device_id={"fsdp": peer(k)}, device_id_type=MESH)

    @pl.when(roots)
    def _():
        for g in range(1, groups):
            pl.semaphore_signal(barrier, inc=1, device_id={"group": g}, device_id_type=MESH)

    locals_[0].start()

    @pl.when(relays)
    def _():
        pl.semaphore_wait(barrier, n)

    @pl.when(jnp.logical_not(relays))
    def _():
        pl.semaphore_wait(barrier, n - 1)

    def hop_copy(m, d):
        return remote(held.at[:, d // 2, :, lanes_of(d)], hop.at[me], hop_s, hop_r, d)

    def got_copy(t, m, d):
        return remote(own.at[:, out_cols(d, t)], got.at[t, share_rows(me)],
                      got_s, got_r.at[t, m // per], d)

    def right_copy(t, m, d):
        src = staged.at[pl.ds(left_groups + (d * halves + t) * block_groups, block_groups)]
        dst = right.at[t, :, rows_of(me), lanes_of(me)]
        return remote(src, dst, right_s, right_r.at[t], d)

    def left_copy(m, d):
        return remote(staged.at[pl.ds(0, left_groups)], left.at[:, rows_of(me), lanes_of(me)],
                      left_s.at[0], left_r.at[0], d)

    locals_[1].wait()
    for pair in order:
        hop_copy(*pick(pair)).start()
    pltpu.make_async_copy(held.at[:, me // 2, :, lanes_of(me)], hop.at[me], hop_r).start()
    for copy in locals_[2:]:
        copy.start()
    shared = left.at[:, :, lanes_of(me)]
    sibling = remote(shared, shared, left_s.at[1], left_r.at[1], peer(1))

    def send_got(t, i=None):
        if i is None:
            pairs = order
        else:
            part = [m for m in masks if m // per == i]
            pairs = [(part[j], part[j + 1 - 2 * (j % 2)]) for j in range(len(part))]
            pairs = pairs + ([] if i else [(1, 1)])
        for pair in pairs:
            got_copy(t, *pick(pair)).start()

    locals_[0].wait()
    squares = jnp.zeros((8, LANES), jnp.float32)
    for r in range(0, share, 16):
        rows = own[r:r + 16, :].astype(jnp.float32)
        rows = rows * rows
        rows = rows[0:8] + rows[8:16]
        for c in range(0, cols, LANES):
            squares = squares + rows[:, c:c + LANES]
    sq_own[...] = squares

    @pl.when(follows)
    def _():
        remote(sq_own, sq_f.at[lax.rem(me + n - LEAD - 1, n)], f_s, f_r, LEAD).start()

    send_got(0)

    @pl.when(leads)
    def _():
        settle(sq_f, f_r)
        squares = sq_own[...]
        for k in range(n - 1):
            squares = squares + sq_f[k]
        sq_mid[...] = squares

    @pl.when(relays)
    def _():
        across(sq_mid, sq_z.at[lax.rem(zz + groups - 1, groups)], 0).start()

    settle(hop, hop_r)
    owner = lax.rem(step[0] + ident[0], n)
    left_shards = -(-left_groups // per_owner)

    def stage(q):
        staged[q * per_owner:(q + 1) * per_owner] = hop[lax.rem(owner + q, n)]

    def send_right(t):
        for pair in order:
            right_copy(t, *pick(pair)).start()

    for q in range(left_shards):
        stage(q)
    for m in [m for m in masks if m % 2 == 0]:
        left_copy(m, peer(m)).start()
    for q in range(left_shards, n):
        stage(q)
    send_right(0)
    pltpu.make_async_copy(
        staged.at[pl.ds(0, left_groups)], left.at[:, rows_of(me), lanes_of(me)],
        left_r.at[0]).start()
    for t in range(halves):
        pltpu.make_async_copy(
            staged.at[pl.ds(left_groups + (me * halves + t) * block_groups, block_groups)],
            right.at[t, :, rows_of(me), lanes_of(me)], right_r.at[t]).start()

    @pl.when(roots)
    def _():
        settle(sq_z, z_r)
        squares = sq_mid[...]
        for k in range(groups - 1):
            squares = squares + sq_z[k]
        sq_all[...] = squares
        for g in range(1, groups):
            across(sq_all, sq_all, g).start()

    @pl.when(relays)
    def _():
        settle(sq_all, z_r)

    @pl.when(leads)
    def _():
        for f in range(n):
            if f != LEAD:
                remote(sq_all, sq_all, f_s, f_r, f).start()

    far = list(range(n - 2, 0, -2))
    late = [p for m in far for p in ((m, m + 1), (m + 1, m))] + [(1, 1)]
    for t in range(1, halves):
        for pair in late:
            got_copy(t, *pick(pair)).start()
        send_right(t)

    count = jnp.full((1, 1), step[0].astype(jnp.float32))
    first_inv = 1.0 / (1.0 - jnp.exp(count * jnp.float32(math.log(BETA_ONE))))
    second_inv = 1.0 / (1.0 - jnp.exp(count * jnp.float32(math.log(BETA_TWO))))

    settle(shared, left_r.at[0])
    sibling.start()
    clip = None
    for t in range(halves):
        settle(right.at[t], right_r.at[t])
        rt = right[t].reshape(BLOCK, BLOCK)
        flipped = rt.astype(jnp.float32).T.astype(jnp.bfloat16)
        cut = slice(t * BLOCK, (t + 1) * BLOCK)
        if t == 0:
            sibling.wait_recv()
        for i in reversed(range(left_blocks)):
            b = peer(i * per) // per
            cols_b = pl.ds(pl.multiple_of(b * BLOCK, BLOCK), BLOCK)
            near = range(i * per, (i + 1) * per)
            settle(got.at[t, cols_b], got_r.at[t, i])
            lb = left[pl.ds(b * block_groups, block_groups)].reshape(BLOCK, BLOCK)
            turned = mm(flipped, got[t, cols_b, :], NT)
            rotated = sum(mm(piece, lb, NN) for piece in pieces_of(turned))
            if clip is None:
                @pl.when(follows)
                def _():
                    settle(sq_all, f_r)

                total = jnp.sum(sq_all[...], keepdims=True)
                clip = jnp.float32(math.sqrt(entries)) / (jnp.sqrt(total) + 1e-06)
                settle(moments, loc.at[1])

            rotated = rotated * clip
            first_sum = BETA_ONE * moments[0, cut, cols_b].astype(jnp.float32) + (1.0 - BETA_ONE) * rotated
            second_sum = (BETA_TWO * moments[1, cut, cols_b].astype(jnp.float32)
                          + (1.0 - BETA_TWO) * rotated * rotated)
            out_1[0, cut, cols_b] = first_sum.astype(jnp.bfloat16)
            out_2[0, cut, cols_b] = second_sum.astype(jnp.bfloat16)
            direction = first_sum * first_inv / (jnp.sqrt(second_sum * second_inv) + ADAM_EPS)
            back = sum(mm(rt, piece, NN) for piece in pieces_of(direction))
            result = sum(mm(lb, piece, NT) for piece in pieces_of(back))
            upd[t, cols_b, :] = result.astype(jnp.bfloat16)
            ahead = [m for m in reversed(near) if m > 1 and m % 2 == 0]
            swap = [m + 1 for m in ahead]
            for pair in list(zip(ahead, swap)) + list(zip(swap, ahead)) + ([] if i else [(1, 1)]):
                d = pick(pair)[1]
                remote(upd.at[t, share_rows(d)], out_u.at[0, :, out_cols(me, t)],
                       ret_s, ret_r, d).start()
            if i == 0:
                pltpu.make_async_copy(upd.at[t, share_rows(me)],
                                      out_u.at[0, :, out_cols(me, t)], ret_r).start()

    settle(hop.at[pl.ds(0, n - 1)], hop_s)

    @pl.when(follows)
    def _():
        settle(sq_own, f_s)

    @pl.when(roots)
    def _():
        settle(sq_z, z_s)

    @pl.when(relays)
    def _():
        settle(sq_mid, z_s)

    @pl.when(leads)
    def _():
        settle(sq_f, f_s)

    settle(staged.at[pl.ds(0, (n // 2 - 1) * left_groups)], left_s.at[0])
    sibling.wait_send()
    settle(staged.at[pl.ds(0, (n - 1) * halves * block_groups)], right_s)
    settle(got.at[:, pl.ds(0, all_rows - share)], got_s)
    settle(upd.at[:, pl.ds(0, all_rows - share)], ret_s)
    settle(out_u, ret_r)


def hbm(x):
    return pltpu.with_memory_space_constraint(x, pltpu.MemorySpace.HBM)


def copy_kernel(a, b, c, x, y, z, sems):
    copies = []
    for src, dst in ((a, x), (b, y), (c, z)):
        rows = src.shape[1] // PARTS
        for i in range(PARTS):
            cut = pl.ds(i * rows, rows)
            copies.append(pltpu.make_async_copy(
                src.at[0, cut], dst.at[0, cut], sems.at[len(copies)]))
    for copy in copies:
        copy.start()
    for copy in copies:
        copy.wait()


def place(arrays):
    return pl.pallas_call(
        copy_kernel,
        out_shape=tuple(jax.ShapeDtypeStruct(a.shape, a.dtype) for a in arrays),
        in_specs=[pl.BlockSpec(memory_space=pltpu.VMEM)] * 3,
        out_specs=(pl.BlockSpec(memory_space=pl.ANY),) * 3,
        scratch_shapes=[pltpu.SemaphoreType.DMA((3 * PARTS,))],
        compiler_params=pltpu.CompilerParams(vmem_limit_bytes=8 << 20),
    )(*arrays)


def fits(gradient, first_moment, basis_store, n):
    if n < 2 or n & (n - 1):
        return False
    span = n // 2 * SLAB
    width = gradient.shape[2] // n
    all_rows = gradient.shape[1] * n
    return (
        BLOCK % span == 0
        and basis_store.shape[1] % span == 0
        and width % BLOCK == 0
        and all_rows % BLOCK == 0
        and n % (all_rows // BLOCK) == 0
        and n // (all_rows // BLOCK) % 2 == 0
        and gradient.shape[1] % SLAB == 0
        and all_rows <= 1024
        and width <= 1024
    )


def local(gradient, first_moment, second_moment, basis_store, step_number, matrix_ids):
    n = lax.axis_size("fsdp")
    groups = lax.axis_size("group")
    if groups < 2 or not fits(gradient, first_moment, basis_store, n):
        return local_general(
            gradient, first_moment, second_moment, basis_store, step_number, matrix_ids
        )
    share, cols = gradient.shape[1:]
    all_rows = share * n
    width = cols // n
    halves = width // BLOCK
    slabs = n // 2
    span = slabs * SLAB
    per_owner = basis_store.shape[1] // span
    basis = basis_store.reshape(per_owner, slabs, SLAB, BLOCK)
    half = jnp.bfloat16
    anywhere = pl.BlockSpec(memory_space=pl.ANY)
    scalar = pl.BlockSpec(memory_space=pltpu.SMEM)
    dma = pltpu.SemaphoreType.DMA
    tile = (8, LANES)
    results = pl.pallas_call(
        functools.partial(kernel, n, groups),
        out_shape=(
            jax.ShapeDtypeStruct(gradient.shape, half),
            jax.ShapeDtypeStruct(first_moment.shape, half),
            jax.ShapeDtypeStruct(second_moment.shape, half),
        ),
        in_specs=[anywhere] * 4 + [scalar] * 2,
        out_specs=(pl.BlockSpec(memory_space=pltpu.VMEM),) * 3,
        scratch_shapes=[
            pltpu.VMEM(basis.shape, half),
            pltpu.VMEM((share, cols), half),
            pltpu.VMEM((2, width, all_rows), half),
            pltpu.VMEM((n, per_owner, SLAB, LANES), half),
            pltpu.VMEM((n * per_owner, SLAB, LANES), half),
            pltpu.VMEM((all_rows // span, span, BLOCK), half),
            pltpu.VMEM((halves, BLOCK // span, span, BLOCK), half),
            pltpu.VMEM((halves, all_rows, BLOCK), half),
            pltpu.VMEM((halves, all_rows, BLOCK), half),
            pltpu.VMEM(tile, jnp.float32),
            pltpu.VMEM((n - 1,) + tile, jnp.float32),
            pltpu.VMEM(tile, jnp.float32),
            pltpu.VMEM((groups - 1,) + tile, jnp.float32),
            pltpu.VMEM(tile, jnp.float32),
            dma((3,)),
            dma(()), dma(()),
            dma((2,)), dma((2,)),
            dma(()), dma((halves,)),
            dma(()), dma((halves, all_rows // BLOCK)),
            dma(()), dma(()),
            dma(()), dma(()),
            dma(()), dma(()),
        ],
        compiler_params=pltpu.CompilerParams(
            collective_id=0, has_side_effects=True, vmem_limit_bytes=32 << 20
        ),
    )(*[hbm(x) for x in (gradient, first_moment, second_moment, basis)], step_number, matrix_ids)
    return place(results)


def solution(mesh):
    in_specs = (
        P("group", "fsdp", None),
        P("group", "fsdp", None),
        P("group", "fsdp", None),
        P("group", "fsdp", None),
        P(),
        P("group"),
    )
    out_specs = (P("group", "fsdp", None), P("group", "fsdp", None), P("group", "fsdp", None))
    return jax.shard_map(local, mesh=mesh, in_specs=in_specs, out_specs=out_specs, check_vma=False)
```
